32 devices in a mesh: chan: 16 (over z, x, core), tm: 2 (over y).
Axes of the slice: x: 2, y: 2, z: 4, core: 2. Of those that a mesh axis runs over, the one named last changes fastest.
Arguments:
- samples: bfloat16 [96, 2, 2048], P('chan', 'tm'), may hold values from -6 to 6
- dead_flags: int32 [96], P('chan'), may hold values 0 or 1
- pair_mask: int32 [96, 96], P('chan', 'tm'), may hold values 0 or 1
Outputs:
- xcorr: float32 [96, 96, 301], P('chan', 'tm')
The draws below stay inside these ranges and needn't reach their ends.
All inputs are finite; a program needn't handle non-finite values. No bound on the sum of `dead_flags` or of `pair_mask` on one device may be relied on, other than what follows from the above.
Results may differ from the reference program's by a relative error of at most 0.0095.
Values may be sent and summed in bfloat16 or wider, within the bound.
A program may use at most 64 MiB of HBM per device.

```python
import math
import jax
import jax.numpy as jnp
from jax import lax

L = 2048
F = 768
LAGS = 301
CHANNELS = 96
SUBWIN = 2


def with_ends(drawn, own_key, low, high):
    extent = drawn.shape
    index_at = [jax.random.randint(jax.random.fold_in(own_key, axis), (), 0, extent[axis]) for axis in range(len(extent))]
    drawn = drawn.at[tuple(index_at)].set(low)
    longest = extent.index(max(extent))
    index_at[longest] = (index_at[longest] + 1) % extent[longest]
    return drawn.at[tuple(index_at)].set(high)


def shard_levels(stream_key, shape, pieces, low, high):
    gain, own = 1.0, jax.random.fold_in(stream_key, 6)
    for axis_at, parts in pieces:
        steps = jnp.exp(jax.random.uniform(jax.random.fold_in(own, axis_at), (parts,), jnp.float32, low / len(pieces), high / len(pieces)))
        gain = gain * jnp.repeat(steps, shape[axis_at] // parts).reshape([-1 if axis == axis_at else 1 for axis in range(len(shape))])
    return gain


def bell_draw(key, extent, deviation, reach, pieces=(), held_as=jnp.bfloat16):
    entries = deviation * jax.random.normal(key, extent, jnp.float32)
    if pieces:
        entries = entries * shard_levels(key, extent, pieces, -0.22, 0.18)
    return jnp.clip(entries, -reach, reach).astype(held_as)


def setup_inputs(seed: int = 0) -> dict:
    splits = jax.random.split(jax.random.key(seed), 4)
    return {
        "samples": bell_draw(splits[0], (CHANNELS, SUBWIN, L), 1.0, 6.0, ((0, 16), (1, 2))),
        "dead_flags": with_ends((jax.random.randint(splits[1], (CHANNELS,), 0, 8) < 1).astype(jnp.int32), jax.random.fold_in(splits[1], 1), 0, 1),
        "pair_mask": with_ends((jax.random.randint(splits[2], (CHANNELS, CHANNELS), 0, 4) < 3).astype(jnp.int32), jax.random.fold_in(splits[2], 1), 0, 1),
    }


def taper_window(length):
    sample_index = jnp.arange(length, dtype=jnp.float32)
    return 0.5 - 0.5 * jnp.cos(2.0 * math.pi * (sample_index + 0.5) / length)

def forward_table(length, bins):
    sample_index = jnp.arange(length, dtype=jnp.int32)
    frequency = jnp.arange(1, bins + 1, dtype=jnp.int32)
    phase_index = sample_index[:, None] * frequency[None, :] % length
    angles = 2.0 * math.pi / length * phase_index.astype(jnp.float32)
    return jnp.concatenate([jnp.cos(angles), -jnp.sin(angles)], axis=1).astype(jnp.bfloat16)

def lag_table(length, bins, lags, factor):
    frequency = jnp.arange(1, bins + 1, dtype=jnp.int32)
    shifts = jnp.arange(lags, dtype=jnp.int32) - (lags - 1) // 2
    phase_index = jnp.mod(frequency[:, None] * shifts[None, :], length)
    angles = 2.0 * math.pi / length * phase_index.astype(jnp.float32)
    table_values = jnp.concatenate([jnp.cos(angles), -jnp.sin(angles)], axis=0) * factor
    return table_values.astype(jnp.bfloat16)

def whiten(samples, dead_flags, table_values):
    channel_count, windows, length = samples.shape
    bins = table_values.shape[1] // 2
    traces = samples.astype(jnp.float32)
    traces = traces - lax.optimization_barrier(jnp.mean(traces, axis=-1, keepdims=True))
    tapered = (traces * taper_window(length)).astype(jnp.bfloat16)
    spectra = jnp.dot(tapered.reshape(channel_count * windows, length), table_values, preferred_element_type=jnp.float32)
    real_part = spectra[:, :bins]
    imag_part = spectra[:, bins:]
    energy = real_part * real_part + imag_part * imag_part
    mean_energy = lax.optimization_barrier(jnp.mean(energy, axis=-1, keepdims=True))
    inverse_scale = lax.rsqrt(energy + 0.25 * mean_energy + 1e-06)
    alive_rows = jnp.repeat((1 - dead_flags).astype(jnp.float32), windows)[:, None]
    whitened = jnp.concatenate([real_part * inverse_scale, imag_part * inverse_scale], axis=1) * alive_rows
    return whitened.astype(jnp.bfloat16).reshape(channel_count, windows, 2 * bins)

def correlate(receivers, sources, lag_weights):
    bins = receivers.shape[-1] // 2
    rec_values = receivers.astype(jnp.float32)
    src_values = sources.astype(jnp.float32)
    rec_re = rec_values[:, None, :, :bins]
    rec_im = rec_values[:, None, :, bins:]
    src_re = src_values[None, :, :, :bins]
    src_im = src_values[None, :, :, bins:]
    cross_re = rec_re * src_re + rec_im * src_im
    cross_im = rec_im * src_re - rec_re * src_im
    cross = jnp.concatenate([cross_re, cross_im], axis=-1).astype(jnp.bfloat16)
    result = jnp.einsum('rgwk,kl->wrgl', cross.astype(jnp.float32), lag_weights.astype(jnp.float32))
    return result.astype(jnp.bfloat16)

def reference(samples, dead_flags, pair_mask):
    channel_count, windows, length = samples.shape
    table_values = forward_table(length, F)
    whitened = whiten(samples, dead_flags, table_values)
    lag_weights = lag_table(length, F, LAGS, 1.0 / math.sqrt(SUBWIN * F))
    block_size = math.gcd(channel_count, 8)
    blocks = whitened.reshape(channel_count // block_size, block_size, windows, 2 * F)

    def one_block(receivers):
        per_window = correlate(receivers, whitened, lag_weights)
        return lax.optimization_barrier(jnp.sum(per_window.astype(jnp.float32), axis=0))
    stacked = lax.map(one_block, blocks).reshape(channel_count, channel_count, LAGS)
    return stacked * pair_mask.astype(jnp.float32)[..., None]
```

```python
import functools
import math

import jax
import jax.numpy as jnp
import numpy as np
from jax import lax
from jax.experimental import pallas as pl
from jax.experimental.pallas import tpu as pltpu
from jax.sharding import PartitionSpec as P

F = 768
LAGS = 301


def taper_window(length):
    sample_index = jnp.arange(length, dtype=jnp.float32)
    return 0.5 - 0.5 * jnp.cos(2.0 * math.pi * (sample_index + 0.5) / length)


def forward_table(length, bins):
    sample_index = jnp.arange(length, dtype=jnp.int32)
    frequency = jnp.arange(1, bins + 1, dtype=jnp.int32)
    phase_index = sample_index[:, None] * frequency[None, :] % length
    angles = 2.0 * math.pi / length * phase_index.astype(jnp.float32)
    return jnp.concatenate([jnp.cos(angles), -jnp.sin(angles)], axis=1).astype(jnp.bfloat16)


def lag_table(length, bins, lags, factor):
    frequency = jnp.arange(1, bins + 1, dtype=jnp.int32)
    shifts = jnp.arange(lags, dtype=jnp.int32) - (lags - 1) // 2
    phase_index = jnp.mod(frequency[:, None] * shifts[None, :], length)
    angles = 2.0 * math.pi / length * phase_index.astype(jnp.float32)
    table_values = jnp.concatenate([jnp.cos(angles), -jnp.sin(angles)], axis=0) * factor
    return table_values.astype(jnp.bfloat16)


def whiten(samples, dead_flags, table_values):
    channel_count, windows, length = samples.shape
    bins = table_values.shape[1] // 2
    traces = samples.astype(jnp.float32)
    traces = traces - jnp.mean(traces, axis=-1, keepdims=True)
    tapered = (traces * taper_window(length)).astype(jnp.bfloat16)
    spectra = jnp.dot(
        tapered.reshape(channel_count * windows, length),
        table_values,
        preferred_element_type=jnp.float32,
    )
    real_part = spectra[:, :bins]
    imag_part = spectra[:, bins:]
    energy = real_part * real_part + imag_part * imag_part
    mean_energy = jnp.mean(energy, axis=-1, keepdims=True)
    inverse_scale = lax.rsqrt(energy + 0.25 * mean_energy + 1e-06)
    alive_rows = jnp.repeat((1 - dead_flags).astype(jnp.float32), windows)[:, None]
    whitened = (
        jnp.concatenate([real_part * inverse_scale, imag_part * inverse_scale], axis=1) * alive_rows
    )
    return whitened.astype(jnp.bfloat16).reshape(channel_count, windows, 2 * bins)


def correlate(receivers, sources, lag_weights):
    bins = receivers.shape[-1] // 2
    rec_values = receivers.astype(jnp.float32)
    src_values = sources.astype(jnp.float32)
    rec_re = rec_values[:, None, :, :bins]
    rec_im = rec_values[:, None, :, bins:]
    src_re = src_values[None, :, :, :bins]
    src_im = src_values[None, :, :, bins:]
    cross_re = rec_re * src_re + rec_im * src_im
    cross_im = rec_im * src_re - rec_re * src_im
    cross = jnp.concatenate([cross_re, cross_im], axis=-1).astype(jnp.bfloat16)
    result = jnp.einsum("rgwk,kl->wrgl", cross, lag_weights, preferred_element_type=jnp.float32)
    return result.astype(jnp.bfloat16)


def pick_group(source_count, rows_each):
    chosen = 1
    for candidate in range(1, source_count + 1):
        if source_count % candidate == 0 and candidate * rows_each <= 1024:
            chosen = candidate
    return chosen


def per_device(samples, dead_flags, pair_mask):
    block_size, local_windows, length = samples.shape
    table_values = forward_table(length, F)
    whitened = whiten(samples, dead_flags, table_values)
    subwin = local_windows * lax.axis_size("tm")
    lag_weights = lag_table(length, F, LAGS, 1.0 / math.sqrt(subwin * F))
    incoming = lax.all_gather(whitened, "chan", axis=0, tiled=True)
    source_count = incoming.shape[0]
    group_size = pick_group(source_count, block_size * local_windows)
    grouped = incoming.reshape(source_count // group_size, group_size, local_windows, 2 * F)

    def one_group(group_sources):
        return correlate(whitened, group_sources, lag_weights)[0]

    results = lax.map(one_group, grouped)
    placed = jnp.transpose(results, (1, 0, 2, 3)).reshape(block_size, source_count, LAGS)
    shares = lax.psum_scatter(
        placed.astype(jnp.float32).astype(jnp.bfloat16), "tm", scatter_dimension=1, tiled=True
    ).astype(jnp.float32)
    return shares * pair_mask.astype(jnp.float32)[..., None]


RADIX = 16
LANES = 128
MESH = pl.DeviceIdType.MESH


def frequency_groups(bins):
    half = RADIX // 2
    groups = []
    for residue in range(half):
        first, second = (0, half) if residue == 0 else (residue, RADIX - residue)
        all_bins = np.arange(1, bins + 1)
        groups.append((first, second, all_bins[all_bins % RADIX == first], all_bins[all_bins % RADIX == second]))
    return groups


def split_tables(length, bins):
    depth = length // RADIX
    offsets = np.arange(depth)
    columns_re, columns_im, owner, order = [], [], [], []
    for index, (first, second, bins_a, bins_b) in enumerate(frequency_groups(bins)):
        for which, chosen in ((0, bins_a), (1, bins_b)):
            for k in chosen:
                angle = 2.0 * np.pi / length * ((offsets * k) % length)
                cos, sin, zero = np.cos(angle), np.sin(angle), np.zeros(depth)
                if index == 0:
                    re = [cos, zero] if which == 0 else [zero, cos]
                    im = [-sin, zero] if which == 0 else [zero, -sin]
                elif which == 0:
                    re, im = [cos, sin], [-sin, cos]
                else:
                    re, im = [cos, -sin], [-sin, -cos]
                columns_re.append(np.concatenate(re))
                columns_im.append(np.concatenate(im))
                owner.append(index)
                order.append(k)
    tiles = bins // LANES
    table = np.zeros((tiles, 4 * depth, 2 * LANES), np.float32)
    reads = []
    for tile in range(tiles):
        owners = sorted(set(owner[tile * LANES : (tile + 1) * LANES]))
        assert len(owners) <= 2
        reads.append(tuple(owners))
        for lane in range(LANES):
            at = tile * LANES + lane
            base = owners.index(owner[at]) * 2 * depth
            table[tile, base : base + 2 * depth, lane] = columns_re[at]
            table[tile, base : base + 2 * depth, LANES + lane] = columns_im[at]
    return table, reads, np.array(order)


def ordered_lag_table(length, order, lags, factor):
    shifts = np.arange(lags) - (lags - 1) // 2
    angles = 2.0 * np.pi / length * np.mod(order[:, None] * shifts[None, :], length)
    values = np.concatenate([np.cos(angles), -np.sin(angles)], axis=0) * factor
    padded = -(-lags // LANES) * LANES
    return np.pad(values, ((0, 0), (0, padded - lags))).astype(np.float32)


def stage_one(pieces):
    half = RADIX // 2
    sums = [pieces[a] + pieces[RADIX - a] for a in range(1, half)]
    diffs = [pieces[a] - pieces[RADIX - a] for a in range(1, half)]
    even = pieces[0] + pieces[half]
    odd = pieces[0] - pieces[half]

    def real(k):
        total = even if k % 2 == 0 else odd
        for a in range(1, half):
            total = total + sums[a - 1] * float(np.cos(2 * np.pi * a * k / RADIX))
        return total

    def imag(k):
        total = diffs[0] * float(-np.sin(2 * np.pi * k / RADIX))
        for a in range(2, half):
            total = total + diffs[a - 1] * float(-np.sin(2 * np.pi * a * k / RADIX))
        return total

    groups = [jnp.concatenate([real(0), real(half)], axis=1)]
    for k in range(1, half):
        groups.append(jnp.concatenate([real(k), imag(k)], axis=1))
    return [g.astype(jnp.bfloat16) for g in groups]


def fused_kernel(
    sizes, reads, samples_ref, dead_ref, taper_ref, table_ref, lag_ref, out_ref,
    own, src, rec, srcf, cross, table, lagv,
    table_sem, send_sem, pair_sem, fwd_sem, src_sem, rec_sem,
):
    chans, tms, block, group, bins = sizes
    me_c, me_t = lax.axis_index("chan"), lax.axis_index("tm")
    core = me_c % 2
    columns = chans // 2
    load_table = pltpu.make_async_copy(table_ref, table, table_sem.at[0])
    load_table.start()
    load_lag = pltpu.make_async_copy(lag_ref, lagv, table_sem.at[1])
    load_lag.start()

    barrier = pltpu.get_barrier_semaphore()
    everyone = columns * tms
    flat = (me_c // 2) * tms + me_t
    for step in range(1, everyone):
        other = (flat + step) % everyone
        pl.semaphore_signal(
            barrier, inc=1, device_id=((other // tms) * 2 + core, other % tms), device_id_type=MESH
        )
    sibling = me_c + 1 - 2 * core
    pl.semaphore_signal(barrier, inc=1, device_id=(sibling, me_t), device_id_type=MESH)

    length = samples_ref.shape[-1]
    depth = length // RADIX
    traces = samples_ref[...].reshape(block, length).astype(jnp.float32)
    traces = traces - jnp.mean(traces, axis=-1, keepdims=True)
    tapered = (traces * taper_ref[...]).astype(jnp.bfloat16).astype(jnp.float32)
    groups = stage_one([tapered[:, a * depth : (a + 1) * depth] for a in range(RADIX)])
    row = lax.broadcasted_iota(jnp.int32, (block, 1), 0)
    alive = jnp.zeros((block, 1), jnp.float32)
    for r in range(block):
        alive = jnp.where(row == r, (1 - dead_ref[r]).astype(jnp.float32), alive)
    load_table.wait()
    parts = []
    energy_sum = jnp.zeros((block, LANES), jnp.float32)
    for tile, owners in enumerate(reads):
        lhs = jnp.concatenate([groups[g] for g in owners], axis=1)
        spec = jnp.dot(lhs, table[tile, : lhs.shape[1], :], preferred_element_type=jnp.float32)
        re, im = spec[:, :LANES], spec[:, LANES:]
        energy = re * re + im * im
        energy_sum = energy_sum + energy
        parts.append((re, im, energy))
    mean_energy = jnp.sum(energy_sum, axis=-1, keepdims=True) / bins
    for tile, (re, im, energy) in enumerate(parts):
        scale = lax.rsqrt(energy + 0.25 * mean_energy + 1e-06)
        lanes = slice(tile * LANES, (tile + 1) * LANES)
        lanes_im = slice(bins + tile * LANES, bins + (tile + 1) * LANES)
        own[:, lanes] = (re * scale * alive).astype(jnp.bfloat16)
        own[:, lanes_im] = (im * scale * alive).astype(jnp.bfloat16)

    pl.semaphore_wait(barrier, everyone)

    to_t = me_c // group
    slot = me_c % group

    def push(column):
        to_c = 2 * column + core
        return pltpu.make_async_remote_copy(
            src_ref=own, dst_ref=src.at[slot, me_t],
            send_sem=send_sem.at[column], recv_sem=src_sem.at[slot, me_t],
            device_id=(to_c, to_t), device_id_type=MESH,
        )

    for column in range(columns):
        is_self = jnp.logical_and(2 * column + core == me_c, to_t == me_t)

        @pl.when(jnp.logical_not(is_self))
        def _():
            push(column).start()

        @pl.when(is_self)
        def _():
            pltpu.make_async_copy(own, src.at[slot, me_t], src_sem.at[slot, me_t]).start()

    def pair_copy(step):
        return pltpu.make_async_remote_copy(
            src_ref=own, dst_ref=rec.at[me_t],
            send_sem=pair_sem.at[step], recv_sem=rec_sem.at[me_t],
            device_id=(me_c, (me_t + step) % tms), device_id_type=MESH,
        )

    for step in range(1, tms):
        pair_copy(step).start()
    own_rec = pltpu.make_async_copy(own, rec.at[me_t], pair_sem.at[0])
    own_rec.start()

    def arrival(b, w):
        return pltpu.make_async_copy(own, src.at[b, w], src_sem.at[b, w])

    def forward(b, w):
        return pltpu.make_async_remote_copy(
            src_ref=src.at[b, w], dst_ref=src.at[b, w],
            send_sem=fwd_sem.at[b, w], recv_sem=src_sem.at[b, w],
            device_id=(sibling, me_t), device_id_type=MESH,
        )

    for half_block in range(group // 2):
        for w in range(tms):
            b = 2 * half_block + core
            arrival(b, w).wait()
            forward(b, w).start()
    own_rec.wait()
    for step in range(1, tms):
        from_t = (me_t + step) % tms
        pltpu.make_async_copy(own, rec.at[from_t], rec_sem.at[from_t]).wait()
    for half_block in range(group // 2):
        for w in range(tms):
            arrival(2 * half_block + 1 - core, w).wait()

    sources = group * block
    for b in range(group):
        for w in range(tms):
            srcf[w, b * block : (b + 1) * block, :] = src[b, w].astype(jnp.float32)
    for tile in range(bins // LANES):
        lanes = slice(tile * LANES, (tile + 1) * LANES)
        lanes_im = slice(bins + tile * LANES, bins + (tile + 1) * LANES)
        rec_re = [rec[w, :, lanes].astype(jnp.float32) for w in range(tms)]
        rec_im = [rec[w, :, lanes_im].astype(jnp.float32) for w in range(tms)]
        src_re = [srcf[w, :, lanes] for w in range(tms)]
        src_im = [srcf[w, :, lanes_im] for w in range(tms)]
        for r in range(block):
            total_re = total_im = None
            for w in range(tms):
                a, c = rec_re[w][r : r + 1, :], rec_im[w][r : r + 1, :]
                now_re = a * src_re[w] + c * src_im[w]
                now_im = c * src_re[w] - a * src_im[w]
                total_re = now_re if total_re is None else total_re + now_re
                total_im = now_im if total_im is None else total_im + now_im
            cross[r * sources : (r + 1) * sources, lanes] = total_re.astype(jnp.bfloat16)
            cross[r * sources : (r + 1) * sources, lanes_im] = total_im.astype(jnp.bfloat16)
    load_lag.wait()
    lags = out_ref.shape[-1]
    for r in range(block):
        result = jnp.dot(
            cross[r * sources : (r + 1) * sources, :], lagv[...], preferred_element_type=jnp.float32
        )
        out_ref[r] = result[:, :lags]

    for column in range(columns):
        is_self = jnp.logical_and(2 * column + core == me_c, to_t == me_t)

        @pl.when(jnp.logical_not(is_self))
        def _():
            push(column).wait_send()

    for step in range(1, tms):
        pair_copy(step).wait_send()
    for half_block in range(group // 2):
        for w in range(tms):
            forward(2 * half_block + core, w).wait_send()


def fused_device(chans, tms, samples, dead_flags, pair_mask):
    block, _, length = samples.shape
    sources = pair_mask.shape[1]
    group = sources // block
    table, reads, order = split_tables(length, F)
    lag_weights = ordered_lag_table(length, order, LAGS, 1.0 / math.sqrt(tms * F))
    at = np.arange(length)
    taper = (0.5 - 0.5 * np.cos(2.0 * np.pi * (at + 0.5) / length))[None, :].astype(np.float32)
    vmem, hbm = pl.BlockSpec(memory_space=pltpu.VMEM), pl.BlockSpec(memory_space=pl.ANY)
    sem = pltpu.SemaphoreType.DMA
    result = pl.pallas_call(
        functools.partial(fused_kernel, (chans, tms, block, group, F), reads),
        out_shape=jax.ShapeDtypeStruct((block, sources, LAGS), jnp.float32),
        in_specs=[vmem, pl.BlockSpec(memory_space=pltpu.SMEM), vmem, hbm, hbm],
        out_specs=vmem,
        scratch_shapes=[
            pltpu.VMEM((block, 2 * F), jnp.bfloat16),
            pltpu.VMEM((group, tms, block, 2 * F), jnp.bfloat16),
            pltpu.VMEM((tms, block, 2 * F), jnp.bfloat16),
            pltpu.VMEM((tms, sources, 2 * F), jnp.float32),
            pltpu.VMEM((block * sources, 2 * F), jnp.bfloat16),
            pltpu.VMEM(table.shape, jnp.bfloat16),
            pltpu.VMEM(lag_weights.shape, jnp.bfloat16),
            sem((2,)), sem((chans // 2,)), sem((tms,)), sem((group, tms)), sem((group, tms)), sem((tms,)),
        ],
        compiler_params=pltpu.CompilerParams(collective_id=0, has_side_effects=True),
    )(
        samples, dead_flags, jnp.asarray(taper),
        jnp.asarray(table, jnp.bfloat16), jnp.asarray(lag_weights, jnp.bfloat16),
    )
    return result * pair_mask.astype(jnp.float32)[..., None]


def dispatch(chans, tms, samples, dead_flags, pair_mask):
    block, windows, length = samples.shape
    sources = pair_mask.shape[1]
    whole_blocks = sources % (2 * block) == 0 and chans % 2 == 0 and sources % 16 == 0
    aligned = length == RADIX * LANES and F % LANES == 0 and windows == 1
    if whole_blocks and aligned:
        return fused_device(chans, tms, samples, dead_flags, pair_mask)
    return per_device(samples, dead_flags, pair_mask)


def solution(mesh):
    in_specs = (P("chan", "tm", None), P("chan"), P("chan", "tm"))
    out_specs = P("chan", "tm", None)
    chans, tms = mesh.shape["chan"], mesh.shape["tm"]
    return jax.shard_map(
        functools.partial(dispatch, chans, tms),
        mesh=mesh, in_specs=in_specs, out_specs=out_specs, check_vma=False,
    )
```

```python
import functools
import math

import jax
import jax.numpy as jnp
import numpy as np
from jax import lax
from jax.experimental import pallas as pl
from jax.experimental.pallas import tpu as pltpu
from jax.sharding import PartitionSpec as P

F = 768
LAGS = 301


def taper_window(length):
    sample_index = jnp.arange(length, dtype=jnp.float32)
    return 0.5 - 0.5 * jnp.cos(2.0 * math.pi * (sample_index + 0.5) / length)


def forward_table(length, bins):
    sample_index = jnp.arange(length, dtype=jnp.int32)
    frequency = jnp.arange(1, bins + 1, dtype=jnp.int32)
    phase_index = sample_index[:, None] * frequency[None, :] % length
    angles = 2.0 * math.pi / length * phase_index.astype(jnp.float32)
    return jnp.concatenate([jnp.cos(angles), -jnp.sin(angles)], axis=1).astype(jnp.bfloat16)


def lag_table(length, bins, lags, factor):
    frequency = jnp.arange(1, bins + 1, dtype=jnp.int32)
    shifts = jnp.arange(lags, dtype=jnp.int32) - (lags - 1) // 2
    phase_index = jnp.mod(frequency[:, None] * shifts[None, :], length)
    angles = 2.0 * math.pi / length * phase_index.astype(jnp.float32)
    table_values = jnp.concatenate([jnp.cos(angles), -jnp.sin(angles)], axis=0) * factor
    return table_values.astype(jnp.bfloat16)


def whiten(samples, dead_flags, table_values):
    channel_count, windows, length = samples.shape
    bins = table_values.shape[1] // 2
    traces = samples.astype(jnp.float32)
    traces = traces - jnp.mean(traces, axis=-1, keepdims=True)
    tapered = (traces * taper_window(length)).astype(jnp.bfloat16)
    spectra = jnp.dot(
        tapered.reshape(channel_count * windows, length),
        table_values,
        preferred_element_type=jnp.float32,
    )
    real_part = spectra[:, :bins]
    imag_part = spectra[:, bins:]
    energy = real_part * real_part + imag_part * imag_part
    mean_energy = jnp.mean(energy, axis=-1, keepdims=True)
    inverse_scale = lax.rsqrt(energy + 0.25 * mean_energy + 1e-06)
    alive_rows = jnp.repeat((1 - dead_flags).astype(jnp.float32), windows)[:, None]
    whitened = (
        jnp.concatenate([real_part * inverse_scale, imag_part * inverse_scale], axis=1) * alive_rows
    )
    return whitened.astype(jnp.bfloat16).reshape(channel_count, windows, 2 * bins)


def correlate(receivers, sources, lag_weights):
    bins = receivers.shape[-1] // 2
    rec_values = receivers.astype(jnp.float32)
    src_values = sources.astype(jnp.float32)
    rec_re = rec_values[:, None, :, :bins]
    rec_im = rec_values[:, None, :, bins:]
    src_re = src_values[None, :, :, :bins]
    src_im = src_values[None, :, :, bins:]
    cross_re = rec_re * src_re + rec_im * src_im
    cross_im = rec_im * src_re - rec_re * src_im
    cross = jnp.concatenate([cross_re, cross_im], axis=-1).astype(jnp.bfloat16)
    result = jnp.einsum("rgwk,kl->wrgl", cross, lag_weights, preferred_element_type=jnp.float32)
    return result.astype(jnp.bfloat16)


def pick_group(source_count, rows_each):
    chosen = 1
    for candidate in range(1, source_count + 1):
        if source_count % candidate == 0 and candidate * rows_each <= 1024:
            chosen = candidate
    return chosen


def per_device(samples, dead_flags, pair_mask):
    block_size, local_windows, length = samples.shape
    table_values = forward_table(length, F)
    whitened = whiten(samples, dead_flags, table_values)
    subwin = local_windows * lax.axis_size("tm")
    lag_weights = lag_table(length, F, LAGS, 1.0 / math.sqrt(subwin * F))
    incoming = lax.all_gather(whitened, "chan", axis=0, tiled=True)
    source_count = incoming.shape[0]
    group_size = pick_group(source_count, block_size * local_windows)
    grouped = incoming.reshape(source_count // group_size, group_size, local_windows, 2 * F)

    def one_group(group_sources):
        return correlate(whitened, group_sources, lag_weights)[0]

    results = lax.map(one_group, grouped)
    placed = jnp.transpose(results, (1, 0, 2, 3)).reshape(block_size, source_count, LAGS)
    shares = lax.psum_scatter(
        placed.astype(jnp.float32).astype(jnp.bfloat16), "tm", scatter_dimension=1, tiled=True
    ).astype(jnp.float32)
    return shares * pair_mask.astype(jnp.float32)[..., None]


RADIX = 16
LANES = 128
MESH = pl.DeviceIdType.MESH


def frequency_groups(bins):
    half = RADIX // 2
    groups = []
    for residue in range(half):
        first, second = (0, half) if residue == 0 else (residue, RADIX - residue)
        all_bins = np.arange(1, bins + 1)
        groups.append((first, second, all_bins[all_bins % RADIX == first], all_bins[all_bins % RADIX == second]))
    return groups


def split_tables(length, bins):
    depth = length // RADIX
    offsets = np.arange(depth)
    columns_re, columns_im, owner, order = [], [], [], []
    for index, (first, second, bins_a, bins_b) in enumerate(frequency_groups(bins)):
        for which, chosen in ((0, bins_a), (1, bins_b)):
            for k in chosen:
                angle = 2.0 * np.pi / length * ((offsets * k) % length)
                cos, sin, zero = np.cos(angle), np.sin(angle), np.zeros(depth)
                if index == 0:
                    re = [cos, zero] if which == 0 else [zero, cos]
                    im = [-sin, zero] if which == 0 else [zero, -sin]
                elif which == 0:
                    re, im = [cos, sin], [-sin, cos]
                else:
                    re, im = [cos, -sin], [-sin, -cos]
                columns_re.append(np.concatenate(re))
                columns_im.append(np.concatenate(im))
                owner.append(index)
                order.append(k)
    tiles = bins // LANES
    table = np.zeros((tiles, 4 * depth, 2 * LANES), np.float32)
    reads = []
    for tile in range(tiles):
        owners = sorted(set(owner[tile * LANES : (tile + 1) * LANES]))
        assert len(owners) <= 2
        reads.append(tuple(owners))
        for lane in range(LANES):
            at = tile * LANES + lane
            base = owners.index(owner[at]) * 2 * depth
            table[tile, base : base + 2 * depth, lane] = columns_re[at]
            table[tile, base : base + 2 * depth, LANES + lane] = columns_im[at]
    return table, reads, np.array(order)


def ordered_lag_table(length, order, lags, factor):
    shifts = np.arange(lags) - (lags - 1) // 2
    angles = 2.0 * np.pi / length * np.mod(order[:, None] * shifts[None, :], length)
    values = np.concatenate([np.cos(angles), -np.sin(angles)], axis=0) * factor
    padded = -(-lags // LANES) * LANES
    return np.pad(values, ((0, 0), (0, padded - lags))).astype(np.float32)


def stage_one(pieces):
    half = RADIX // 2
    sums = [pieces[a] + pieces[RADIX - a] for a in range(1, half)]
    diffs = [pieces[a] - pieces[RADIX - a] for a in range(1, half)]
    even = pieces[0] + pieces[half]
    odd = pieces[0] - pieces[half]

    def real(k):
        total = even if k % 2 == 0 else odd
        for a in range(1, half):
            total = total + sums[a - 1] * float(np.cos(2 * np.pi * a * k / RADIX))
        return total

    def imag(k):
        total = diffs[0] * float(-np.sin(2 * np.pi * k / RADIX))
        for a in range(2, half):
            total = total + diffs[a - 1] * float(-np.sin(2 * np.pi * a * k / RADIX))
        return total

    groups = [jnp.concatenate([real(0), real(half)], axis=1)]
    for k in range(1, half):
        groups.append(jnp.concatenate([real(k), imag(k)], axis=1))
    return [g.astype(jnp.bfloat16) for g in groups]


def fused_kernel(
    sizes, reads, samples_hbm, dead_hbm, taper_hbm, table_ref, lag_ref, out_ref,
    samples_ref, dead_ref, taper_ref, own, src, rec, srcf, cross, table, lagv,
    outv, table_sem, send_sem, pair_sem, fwd_sem, src_sem, rec_sem, out_sem,
):
    chans, tms, block, group, bins = sizes
    me_c, me_t = lax.axis_index("chan"), lax.axis_index("tm")
    core = me_c % 2
    columns = chans // 2
    load_samples = pltpu.make_async_copy(samples_hbm, samples_ref, table_sem.at[2])
    load_samples.start()
    load_dead = pltpu.make_async_copy(dead_hbm, dead_ref, table_sem.at[4])
    load_dead.start()
    load_taper = pltpu.make_async_copy(taper_hbm, taper_ref, table_sem.at[3])
    load_taper.start()
    load_table = pltpu.make_async_copy(table_ref, table, table_sem.at[0])
    load_table.start()
    load_lag = pltpu.make_async_copy(lag_ref, lagv, table_sem.at[1])
    load_lag.start()

    barrier = pltpu.get_barrier_semaphore()
    everyone = columns * tms
    flat = (me_c // 2) * tms + me_t
    for step in range(1, everyone):
        other = (flat + step) % everyone
        pl.semaphore_signal(
            barrier, inc=1, device_id=((other // tms) * 2 + core, other % tms), device_id_type=MESH
        )
    sibling = me_c + 1 - 2 * core
    pl.semaphore_signal(barrier, inc=1, device_id=(sibling, me_t), device_id_type=MESH)

    length = samples_ref.shape[-1]
    depth = length // RADIX
    load_samples.wait()
    load_taper.wait()
    traces = samples_ref[...].astype(jnp.float32)
    traces = traces - jnp.mean(traces, axis=-1, keepdims=True)
    tapered = (traces * taper_ref[...]).astype(jnp.bfloat16).astype(jnp.float32)
    groups = stage_one([tapered[:, a * depth : (a + 1) * depth] for a in range(RADIX)])
    load_dead.wait()
    row = lax.broadcasted_iota(jnp.int32, (block, 1), 0)
    alive = jnp.zeros((block, 1), jnp.float32)
    for r in range(block):
        alive = jnp.where(row == r, (1 - dead_ref[r]).astype(jnp.float32), alive)
    load_table.wait()
    parts = []
    energy_sum = jnp.zeros((block, LANES), jnp.float32)
    for tile, owners in enumerate(reads):
        lhs = jnp.concatenate([groups[g] for g in owners], axis=1)
        spec = jnp.dot(lhs, table[tile, : lhs.shape[1], :], preferred_element_type=jnp.float32)
        re, im = spec[:, :LANES], spec[:, LANES:]
        energy = re * re + im * im
        energy_sum = energy_sum + energy
        parts.append((re, im, energy))
    mean_energy = jnp.sum(energy_sum, axis=-1, keepdims=True) / bins
    for tile, (re, im, energy) in enumerate(parts):
        scale = lax.rsqrt(energy + 0.25 * mean_energy + 1e-06)
        lanes = slice(tile * LANES, (tile + 1) * LANES)
        lanes_im = slice(bins + tile * LANES, bins + (tile + 1) * LANES)
        own[:, lanes] = (re * scale * alive).astype(jnp.bfloat16)
        own[:, lanes_im] = (im * scale * alive).astype(jnp.bfloat16)

    pl.semaphore_wait(barrier, everyone)

    to_t = me_c // group
    slot = me_c % group

    def push(column):
        to_c = 2 * column + core
        return pltpu.make_async_remote_copy(
            src_ref=own, dst_ref=src.at[slot, me_t],
            send_sem=send_sem.at[column], recv_sem=src_sem.at[slot, me_t],
            device_id=(to_c, to_t), device_id_type=MESH,
        )

    for column in range(columns):
        is_self = jnp.logical_and(2 * column + core == me_c, to_t == me_t)

        @pl.when(jnp.logical_not(is_self))
        def _():
            push(column).start()

        @pl.when(is_self)
        def _():
            pltpu.make_async_copy(own, src.at[slot, me_t], src_sem.at[slot, me_t]).start()

    def pair_copy(step):
        return pltpu.make_async_remote_copy(
            src_ref=own, dst_ref=rec.at[me_t],
            send_sem=pair_sem.at[step], recv_sem=rec_sem.at[me_t],
            device_id=(me_c, (me_t + step) % tms), device_id_type=MESH,
        )

    for step in range(1, tms):
        pair_copy(step).start()
    own_rec = pltpu.make_async_copy(own, rec.at[me_t], pair_sem.at[0])
    own_rec.start()

    def arrival(b, w):
        return pltpu.make_async_copy(own, src.at[b, w], src_sem.at[b, w])

    def forward(b, w):
        return pltpu.make_async_remote_copy(
            src_ref=src.at[b, w], dst_ref=src.at[b, w],
            send_sem=fwd_sem.at[b, w], recv_sem=src_sem.at[b, w],
            device_id=(sibling, me_t), device_id_type=MESH,
        )

    for half_block in range(group // 2):
        for w in range(tms):
            b = 2 * half_block + core
            arrival(b, w).wait()
            forward(b, w).start()
    own_rec.wait()
    for step in range(1, tms):
        from_t = (me_t + step) % tms
        pltpu.make_async_copy(own, rec.at[from_t], rec_sem.at[from_t]).wait()
    for half_block in range(group // 2):
        for w in range(tms):
            arrival(2 * half_block + 1 - core, w).wait()

    sources = group * block
    for b in range(group):
        for w in range(tms):
            srcf[w, b * block : (b + 1) * block, :] = src[b, w].astype(jnp.float32)
    for tile in range(bins // LANES):
        lanes = slice(tile * LANES, (tile + 1) * LANES)
        lanes_im = slice(bins + tile * LANES, bins + (tile + 1) * LANES)
        rec_re = [rec[w, :, lanes].astype(jnp.float32) for w in range(tms)]
        rec_im = [rec[w, :, lanes_im].astype(jnp.float32) for w in range(tms)]
        src_re = [srcf[w, :, lanes] for w in range(tms)]
        src_im = [srcf[w, :, lanes_im] for w in range(tms)]
        for r in range(block):
            total_re = total_im = None
            for w in range(tms):
                a, c = rec_re[w][r : r + 1, :], rec_im[w][r : r + 1, :]
                now_re = a * src_re[w] + c * src_im[w]
                now_im = c * src_re[w] - a * src_im[w]
                total_re = now_re if total_re is None else total_re + now_re
                total_im = now_im if total_im is None else total_im + now_im
            cross[r * sources : (r + 1) * sources, lanes] = total_re.astype(jnp.bfloat16)
            cross[r * sources : (r + 1) * sources, lanes_im] = total_im.astype(jnp.bfloat16)
    load_lag.wait()
    lags = out_ref.shape[-1]
    for r in range(block):
        result = jnp.dot(
            cross[r * sources : (r + 1) * sources, :], lagv[...], preferred_element_type=jnp.float32
        )
        outv[r] = result[:, :lags]
        pltpu.make_async_copy(outv.at[r], out_ref.at[r], out_sem.at[r]).start()

    for r in range(block):
        pltpu.make_async_copy(outv.at[r], out_ref.at[r], out_sem.at[r]).wait()
    for column in range(columns):
        is_self = jnp.logical_and(2 * column + core == me_c, to_t == me_t)

        @pl.when(jnp.logical_not(is_self))
        def _():
            push(column).wait_send()

    for step in range(1, tms):
        pair_copy(step).wait_send()
    for half_block in range(group // 2):
        for w in range(tms):
            forward(2 * half_block + core, w).wait_send()


def fused_device(chans, tms, samples, dead_flags, pair_mask):
    block, _, length = samples.shape
    sources = pair_mask.shape[1]
    group = sources // block
    table, reads, order = split_tables(length, F)
    lag_weights = ordered_lag_table(length, order, LAGS, 1.0 / math.sqrt(tms * F))
    at = np.arange(length)
    taper = (0.5 - 0.5 * np.cos(2.0 * np.pi * (at + 0.5) / length))[None, :].astype(np.float32)
    anywhere, hbm = pl.BlockSpec(memory_space=pl.ANY), pl.BlockSpec(memory_space=pltpu.HBM)
    sem = pltpu.SemaphoreType.DMA
    result = pl.pallas_call(
        functools.partial(fused_kernel, (chans, tms, block, group, F), reads),
        out_shape=jax.ShapeDtypeStruct((block, sources, LAGS), jnp.float32),
        in_specs=[hbm] * 5,
        out_specs=anywhere,
        scratch_shapes=[
            pltpu.VMEM((block, length), jnp.bfloat16),
            pltpu.SMEM((block,), jnp.int32),
            pltpu.VMEM((1, length), jnp.float32),
            pltpu.VMEM((block, 2 * F), jnp.bfloat16),
            pltpu.VMEM((group, tms, block, 2 * F), jnp.bfloat16),
            pltpu.VMEM((tms, block, 2 * F), jnp.bfloat16),
            pltpu.VMEM((tms, sources, 2 * F), jnp.float32),
            pltpu.VMEM((block * sources, 2 * F), jnp.bfloat16),
            pltpu.VMEM(table.shape, jnp.bfloat16),
            pltpu.VMEM(lag_weights.shape, jnp.bfloat16),
            pltpu.VMEM((block, sources, LAGS), jnp.float32),
            sem((5,)), sem((chans // 2,)), sem((tms,)), sem((group, tms)), sem((group, tms)), sem((tms,)), sem((block,)),
        ],
        compiler_params=pltpu.CompilerParams(collective_id=0, has_side_effects=True, vmem_limit_bytes=24 * 1024 * 1024),
    )(
        *(
            pltpu.with_memory_space_constraint(operand, pltpu.HBM)
            for operand in (
                samples.reshape(block, length), dead_flags, jnp.asarray(taper),
                jnp.asarray(table, jnp.bfloat16), jnp.asarray(lag_weights, jnp.bfloat16),
            )
        )
    )
    return result * pair_mask.astype(jnp.float32)[..., None]


def dispatch(chans, tms, samples, dead_flags, pair_mask):
    block, windows, length = samples.shape
    sources = pair_mask.shape[1]
    whole_blocks = sources % (2 * block) == 0 and chans % 2 == 0 and sources % 16 == 0
    aligned = length == RADIX * LANES and F % LANES == 0 and windows == 1
    if whole_blocks and aligned:
        return fused_device(chans, tms, samples, dead_flags, pair_mask)
    return per_device(samples, dead_flags, pair_mask)


def solution(mesh):
    in_specs = (P("chan", "tm", None), P("chan"), P("chan", "tm"))
    out_specs = P("chan", "tm", None)
    chans, tms = mesh.shape["chan"], mesh.shape["tm"]
    return jax.shard_map(
        functools.partial(dispatch, chans, tms),
        mesh=mesh, in_specs=in_specs, out_specs=out_specs, check_vma=False,
    )
```

```python
import functools
import math

import jax
import jax.numpy as jnp
import numpy as np
from jax import lax
from jax.experimental import pallas as pl
from jax.experimental.pallas import tpu as pltpu
from jax.sharding import PartitionSpec as P

F = 768
LAGS = 301


def taper_window(length):
    sample_index = jnp.arange(length, dtype=jnp.float32)
    return 0.5 - 0.5 * jnp.cos(2.0 * math.pi * (sample_index + 0.5) / length)


def forward_table(length, bins):
    sample_index = jnp.arange(length, dtype=jnp.int32)
    frequency = jnp.arange(1, bins + 1, dtype=jnp.int32)
    phase_index = sample_index[:, None] * frequency[None, :] % length
    angles = 2.0 * math.pi / length * phase_index.astype(jnp.float32)
    return jnp.concatenate([jnp.cos(angles), -jnp.sin(angles)], axis=1).astype(jnp.bfloat16)


def lag_table(length, bins, lags, factor):
    frequency = jnp.arange(1, bins + 1, dtype=jnp.int32)
    shifts = jnp.arange(lags, dtype=jnp.int32) - (lags - 1) // 2
    phase_index = jnp.mod(frequency[:, None] * shifts[None, :], length)
    angles = 2.0 * math.pi / length * phase_index.astype(jnp.float32)
    table_values = jnp.concatenate([jnp.cos(angles), -jnp.sin(angles)], axis=0) * factor
    return table_values.astype(jnp.bfloat16)


def whiten(samples, dead_flags, table_values):
    channel_count, windows, length = samples.shape
    bins = table_values.shape[1] // 2
    traces = samples.astype(jnp.float32)
    traces = traces - jnp.mean(traces, axis=-1, keepdims=True)
    tapered = (traces * taper_window(length)).astype(jnp.bfloat16)
    spectra = jnp.dot(
        tapered.reshape(channel_count * windows, length),
        table_values,
        preferred_element_type=jnp.float32,
    )
    real_part = spectra[:, :bins]
    imag_part = spectra[:, bins:]
    energy = real_part * real_part + imag_part * imag_part
    mean_energy = jnp.mean(energy, axis=-1, keepdims=True)
    inverse_scale = lax.rsqrt(energy + 0.25 * mean_energy + 1e-06)
    alive_rows = jnp.repeat((1 - dead_flags).astype(jnp.float32), windows)[:, None]
    whitened = (
        jnp.concatenate([real_part * inverse_scale, imag_part * inverse_scale], axis=1) * alive_rows
    )
    return whitened.astype(jnp.bfloat16).reshape(channel_count, windows, 2 * bins)


def correlate(receivers, sources, lag_weights):
    bins = receivers.shape[-1] // 2
    rec_values = receivers.astype(jnp.float32)
    src_values = sources.astype(jnp.float32)
    rec_re = rec_values[:, None, :, :bins]
    rec_im = rec_values[:, None, :, bins:]
    src_re = src_values[None, :, :, :bins]
    src_im = src_values[None, :, :, bins:]
    cross_re = rec_re * src_re + rec_im * src_im
    cross_im = rec_im * src_re - rec_re * src_im
    cross = jnp.concatenate([cross_re, cross_im], axis=-1).astype(jnp.bfloat16)
    result = jnp.einsum("rgwk,kl->wrgl", cross, lag_weights, preferred_element_type=jnp.float32)
    return result.astype(jnp.bfloat16)


def pick_group(source_count, rows_each):
    chosen = 1
    for candidate in range(1, source_count + 1):
        if source_count % candidate == 0 and candidate * rows_each <= 1024:
            chosen = candidate
    return chosen


def per_device(samples, dead_flags, pair_mask):
    block_size, local_windows, length = samples.shape
    table_values = forward_table(length, F)
    whitened = whiten(samples, dead_flags, table_values)
    subwin = local_windows * lax.axis_size("tm")
    lag_weights = lag_table(length, F, LAGS, 1.0 / math.sqrt(subwin * F))
    incoming = lax.all_gather(whitened, "chan", axis=0, tiled=True)
    source_count = incoming.shape[0]
    group_size = pick_group(source_count, block_size * local_windows)
    grouped = incoming.reshape(source_count // group_size, group_size, local_windows, 2 * F)

    def one_group(group_sources):
        return correlate(whitened, group_sources, lag_weights)[0]

    results = lax.map(one_group, grouped)
    placed = jnp.transpose(results, (1, 0, 2, 3)).reshape(block_size, source_count, LAGS)
    shares = lax.psum_scatter(
        placed.astype(jnp.float32).astype(jnp.bfloat16), "tm", scatter_dimension=1, tiled=True
    ).astype(jnp.float32)
    return shares * pair_mask.astype(jnp.float32)[..., None]


RADIX = 16
LANES = 128
MESH = pl.DeviceIdType.MESH


def frequency_groups(bins):
    half = RADIX // 2
    groups = []
    for residue in range(half):
        first, second = (0, half) if residue == 0 else (residue, RADIX - residue)
        all_bins = np.arange(1, bins + 1)
        groups.append((first, second, all_bins[all_bins % RADIX == first], all_bins[all_bins % RADIX == second]))
    return groups


def split_tables(length, bins):
    depth = length // RADIX
    offsets = np.arange(depth)
    columns_re, columns_im, owner, order = [], [], [], []
    for index, (first, second, bins_a, bins_b) in enumerate(frequency_groups(bins)):
        for which, chosen in ((0, bins_a), (1, bins_b)):
            for k in chosen:
                angle = 2.0 * np.pi / length * ((offsets * k) % length)
                cos, sin, zero = np.cos(angle), np.sin(angle), np.zeros(depth)
                if index == 0:
                    re = [cos, zero] if which == 0 else [zero, cos]
                    im = [-sin, zero] if which == 0 else [zero, -sin]
                elif which == 0:
                    re, im = [cos, sin], [-sin, cos]
                else:
                    re, im = [cos, -sin], [-sin, -cos]
                columns_re.append(np.concatenate(re))
                columns_im.append(np.concatenate(im))
                owner.append(index)
                order.append(k)
    tiles = bins // LANES
    table = np.zeros((tiles, 4 * depth, 2 * LANES), np.float32)
    reads = []
    for tile in range(tiles):
        owners = sorted(set(owner[tile * LANES : (tile + 1) * LANES]))
        assert len(owners) <= 2
        reads.append(tuple(owners))
        for lane in range(LANES):
            at = tile * LANES + lane
            base = owners.index(owner[at]) * 2 * depth
            table[tile, base : base + 2 * depth, lane] = columns_re[at]
            table[tile, base : base + 2 * depth, LANES + lane] = columns_im[at]
    return table, reads, np.array(order)


def ordered_lag_table(length, order, lags, factor):
    shifts = np.arange(lags) - (lags - 1) // 2
    angles = 2.0 * np.pi / length * np.mod(order[:, None] * shifts[None, :], length)
    values = np.concatenate([np.cos(angles), -np.sin(angles)], axis=0) * factor
    padded = -(-lags // LANES) * LANES
    return np.pad(values, ((0, 0), (0, padded - lags))).astype(np.float32)


def stage_one(pieces):
    half = RADIX // 2
    sums = [pieces[a] + pieces[RADIX - a] for a in range(1, half)]
    diffs = [pieces[a] - pieces[RADIX - a] for a in range(1, half)]
    even = pieces[0] + pieces[half]
    odd = pieces[0] - pieces[half]

    def real(k):
        total = even if k % 2 == 0 else odd
        for a in range(1, half):
            total = total + sums[a - 1] * float(np.cos(2 * np.pi * a * k / RADIX))
        return total

    def imag(k):
        total = diffs[0] * float(-np.sin(2 * np.pi * k / RADIX))
        for a in range(2, half):
            total = total + diffs[a - 1] * float(-np.sin(2 * np.pi * a * k / RADIX))
        return total

    groups = [jnp.concatenate([real(0), real(half)], axis=1)]
    for k in range(1, half):
        groups.append(jnp.concatenate([real(k), imag(k)], axis=1))
    return [g.astype(jnp.bfloat16) for g in groups]


def fused_kernel(
    sizes, reads, samples_hbm, dead_hbm, mask_hbm, taper_hbm, table_ref, lag_ref, out_ref, keep_ref,
    samples_ref, dead_ref, maskv, taper_ref, own, src, rec, srcf, cross, table, lagv,
    table_sem, send_sem, pair_sem, fwd_sem, src_sem, rec_sem,
):
    chans, tms, block, group, bins = sizes
    me_c, me_t = lax.axis_index("chan"), lax.axis_index("tm")
    core = me_c % 2
    columns = chans // 2
    load_samples = pltpu.make_async_copy(samples_hbm, samples_ref, table_sem.at[2])
    load_samples.start()
    load_dead = pltpu.make_async_copy(dead_hbm, dead_ref, table_sem.at[4])
    load_dead.start()
    load_mask = pltpu.make_async_copy(mask_hbm, maskv, table_sem.at[5])
    load_mask.start()
    load_taper = pltpu.make_async_copy(taper_hbm, taper_ref, table_sem.at[3])
    load_taper.start()
    load_table = pltpu.make_async_copy(table_ref, table, table_sem.at[0])
    load_table.start()
    load_lag = pltpu.make_async_copy(lag_ref, lagv, table_sem.at[1])
    load_lag.start()

    barrier = pltpu.get_barrier_semaphore()
    sibling = me_c + 1 - 2 * core
    half = group // 2
    for i in range(half):
        for w in range(tms):
            from_c = me_t * group + core * half + i

            @pl.when(jnp.logical_not(jnp.logical_and(from_c == me_c, w == me_t)))
            def _():
                pl.semaphore_signal(barrier, inc=1, device_id=(from_c, w), device_id_type=MESH)

    for step in range(1, tms):
        pl.semaphore_signal(
            barrier, inc=1, device_id=(me_c, (me_t + step) % tms), device_id_type=MESH
        )
    pl.semaphore_signal(barrier, inc=1, device_id=(sibling, me_t), device_id_type=MESH)

    length = samples_ref.shape[-1]
    depth = length // RADIX
    load_samples.wait()
    load_taper.wait()
    traces = samples_ref[...].astype(jnp.float32)
    traces = traces - jnp.mean(traces, axis=-1, keepdims=True)
    tapered = (traces * taper_ref[...]).astype(jnp.bfloat16).astype(jnp.float32)
    groups = stage_one([tapered[:, a * depth : (a + 1) * depth] for a in range(RADIX)])
    load_dead.wait()
    row = lax.broadcasted_iota(jnp.int32, (block, 1), 0)
    alive = jnp.zeros((block, 1), jnp.float32)
    for r in range(block):
        alive = jnp.where(row == r, (1 - dead_ref[r]).astype(jnp.float32), alive)
    load_table.wait()
    parts = []
    energy_sum = jnp.zeros((block, LANES), jnp.float32)
    for tile, owners in enumerate(reads):
        lhs = jnp.concatenate([groups[g] for g in owners], axis=1)
        spec = jnp.dot(lhs, table[tile, : lhs.shape[1], :], preferred_element_type=jnp.float32)
        re, im = spec[:, :LANES], spec[:, LANES:]
        energy = re * re + im * im
        energy_sum = energy_sum + energy
        parts.append((re, im, energy))
    mean_energy = jnp.sum(energy_sum, axis=-1, keepdims=True) / bins
    for tile, (re, im, energy) in enumerate(parts):
        scale = lax.rsqrt(energy + 0.25 * mean_energy + 1e-06)
        lanes = slice(tile * LANES, (tile + 1) * LANES)
        lanes_im = slice(bins + tile * LANES, bins + (tile + 1) * LANES)
        own[:, lanes] = (re * scale * alive).astype(jnp.bfloat16)
        own[:, lanes_im] = (im * scale * alive).astype(jnp.bfloat16)

    to_t = me_c // group
    slot = me_c % group
    to_half, at = slot // half, slot % half
    keeps = jnp.logical_and(to_t == me_t, to_half == core)
    pl.semaphore_wait(barrier, columns + tms - keeps.astype(jnp.int32))

    def column_at(i):
        return (me_c // 2 + columns // 2 + i) % columns

    def stays(i):
        return jnp.logical_and(keeps, column_at(i) == me_c // 2)

    def push(i):
        return pltpu.make_async_remote_copy(
            src_ref=own, dst_ref=src.at[to_half, at, me_t],
            send_sem=send_sem.at[i], recv_sem=src_sem.at[to_half, at, me_t],
            device_id=(2 * column_at(i) + to_half, to_t), device_id_type=MESH,
        )

    for i in range(columns):

        @pl.when(jnp.logical_not(stays(i)))
        def _():
            push(i).start()

        @pl.when(stays(i))
        def _():
            pltpu.make_async_copy(own, src.at[to_half, at, me_t], src_sem.at[to_half, at, me_t]).start()

    def pair_copy(step):
        return pltpu.make_async_remote_copy(
            src_ref=own, dst_ref=rec.at[me_t],
            send_sem=pair_sem.at[step], recv_sem=rec_sem.at[me_t],
            device_id=(me_c, (me_t + step) % tms), device_id_type=MESH,
        )

    for step in range(1, tms):
        pair_copy(step).start()
    own_rec = pltpu.make_async_copy(own, rec.at[me_t], pair_sem.at[0])
    own_rec.start()

    def arrival(h, i, w):
        return pltpu.make_async_copy(own, src.at[h, i, w], src_sem.at[h, i, w])

    def forward(i, w):
        return pltpu.make_async_remote_copy(
            src_ref=src.at[core, i, w], dst_ref=src.at[core, i, w],
            send_sem=fwd_sem.at[i, w], recv_sem=src_sem.at[core, i, w],
            device_id=(sibling, me_t), device_id_type=MESH,
        )

    sources = half * block
    lags = out_ref.shape[-1]

    def correlate_half(h):
        for i in range(half):
            for w in range(tms):
                srcf[w, i * block : (i + 1) * block, :] = src[h, i, w].astype(jnp.float32)
        for tile in range(bins // LANES):
            lanes = slice(tile * LANES, (tile + 1) * LANES)
            lanes_im = slice(bins + tile * LANES, bins + (tile + 1) * LANES)
            rec_re = [rec[w, :, lanes].astype(jnp.float32) for w in range(tms)]
            rec_im = [rec[w, :, lanes_im].astype(jnp.float32) for w in range(tms)]
            src_re = [srcf[w, :, lanes] for w in range(tms)]
            src_im = [srcf[w, :, lanes_im] for w in range(tms)]
            for r in range(block):
                total_re = total_im = None
                for w in range(tms):
                    a, c = rec_re[w][r : r + 1, :], rec_im[w][r : r + 1, :]
                    now_re = a * src_re[w] + c * src_im[w]
                    now_im = c * src_re[w] - a * src_im[w]
                    total_re = now_re if total_re is None else total_re + now_re
                    total_im = now_im if total_im is None else total_im + now_im
                cross[r * sources : (r + 1) * sources, lanes] = total_re.astype(jnp.bfloat16)
                cross[r * sources : (r + 1) * sources, lanes_im] = total_im.astype(jnp.bfloat16)
        result = jnp.dot(cross[...], lagv[...], preferred_element_type=jnp.float32)
        for r in range(block):
            out_ref[r, pl.ds(pl.multiple_of(h * sources, sources), sources), :] = result[
                r * sources : (r + 1) * sources, :lags
            ]

    for i in range(half):
        for w in range(tms):
            arrival(core, i, w).wait()
            forward(i, w).start()
    load_mask.wait()
    keep_ref[...] = maskv[...].astype(jnp.float32)
    load_lag.wait()
    own_rec.wait()
    for step in range(1, tms):
        from_t = (me_t + step) % tms
        pltpu.make_async_copy(own, rec.at[from_t], rec_sem.at[from_t]).wait()

    @pl.loop(0, 2)
    def _(turn):
        @pl.when(turn == 1)
        def _():
            for i in range(half):
                for w in range(tms):
                    arrival(1 - core, i, w).wait()

        correlate_half((core + turn) % 2)

    for i in range(columns):

        @pl.when(jnp.logical_not(stays(i)))
        def _():
            push(i).wait_send()

    for step in range(1, tms):
        pair_copy(step).wait_send()
    for i in range(half):
        for w in range(tms):
            forward(i, w).wait_send()


def fused_device(chans, tms, samples, dead_flags, pair_mask):
    block, _, length = samples.shape
    sources = pair_mask.shape[1]
    group = sources // block
    table, reads, order = split_tables(length, F)
    lag_weights = ordered_lag_table(length, order, LAGS, 1.0 / math.sqrt(tms * F))
    at = np.arange(length)
    taper = (0.5 - 0.5 * np.cos(2.0 * np.pi * (at + 0.5) / length))[None, :].astype(np.float32)
    vmem, hbm = pl.BlockSpec(memory_space=pltpu.VMEM), pl.BlockSpec(memory_space=pltpu.HBM)
    sem = pltpu.SemaphoreType.DMA
    half = group // 2
    result, keep = pl.pallas_call(
        functools.partial(fused_kernel, (chans, tms, block, group, F), reads),
        out_shape=[
            pltpu.VMEM((block, sources, LAGS), jnp.float32),
            pltpu.VMEM((block, sources), jnp.float32),
        ],
        in_specs=[hbm] * 6,
        out_specs=[vmem] * 2,
        scratch_shapes=[
            pltpu.VMEM((block, length), jnp.bfloat16),
            pltpu.SMEM((block,), jnp.int32),
            pltpu.VMEM((block, sources), jnp.int32),
            pltpu.VMEM((1, length), jnp.float32),
            pltpu.VMEM((block, 2 * F), jnp.bfloat16),
            pltpu.VMEM((2, half, tms, block, 2 * F), jnp.bfloat16),
            pltpu.VMEM((tms, block, 2 * F), jnp.bfloat16),
            pltpu.VMEM((tms, half * block, 2 * F), jnp.float32),
            pltpu.VMEM((block * half * block, 2 * F), jnp.bfloat16),
            pltpu.VMEM(table.shape, jnp.bfloat16),
            pltpu.VMEM(lag_weights.shape, jnp.bfloat16),
            sem((6,)), sem((chans // 2,)), sem((tms,)), sem((half, tms)), sem((2, half, tms)), sem((tms,)),
        ],
        compiler_params=pltpu.CompilerParams(
            collective_id=0, has_side_effects=True, vmem_limit_bytes=24 * 1024 * 1024
        ),
    )(
        *(
            pltpu.with_memory_space_constraint(operand, pltpu.HBM)
            for operand in (
                samples.reshape(block, length), dead_flags, pair_mask, jnp.asarray(taper),
                jnp.asarray(table, jnp.bfloat16), jnp.asarray(lag_weights, jnp.bfloat16),
            )
        )
    )
    return result * keep[..., None]


def dispatch(chans, tms, samples, dead_flags, pair_mask):
    block, windows, length = samples.shape
    sources = pair_mask.shape[1]
    whole_blocks = sources % (2 * block) == 0 and chans % 2 == 0 and sources % 16 == 0 and block * chans == sources * tms
    aligned = length == RADIX * LANES and F % LANES == 0 and windows == 1
    if whole_blocks and aligned:
        return fused_device(chans, tms, samples, dead_flags, pair_mask)
    return per_device(samples, dead_flags, pair_mask)


def solution(mesh):
    in_specs = (P("chan", "tm", None), P("chan"), P("chan", "tm"))
    out_specs = P("chan", "tm", None)
    chans, tms = mesh.shape["chan"], mesh.shape["tm"]
    return jax.shard_map(
        functools.partial(dispatch, chans, tms),
        mesh=mesh, in_specs=in_specs, out_specs=out_specs, check_vma=False,
    )
```

```python
import functools
import math

import jax
import jax.numpy as jnp
import numpy as np
from jax import lax
from jax.experimental import pallas as pl
from jax.experimental.pallas import tpu as pltpu
from jax.sharding import PartitionSpec as P

F = 768
LAGS = 301


def taper_window(length):
    sample_index = jnp.arange(length, dtype=jnp.float32)
    return 0.5 - 0.5 * jnp.cos(2.0 * math.pi * (sample_index + 0.5) / length)


def forward_table(length, bins):
    sample_index = jnp.arange(length, dtype=jnp.int32)
    frequency = jnp.arange(1, bins + 1, dtype=jnp.int32)
    phase_index = sample_index[:, None] * frequency[None, :] % length
    angles = 2.0 * math.pi / length * phase_index.astype(jnp.float32)
    return jnp.concatenate([jnp.cos(angles), -jnp.sin(angles)], axis=1).astype(jnp.bfloat16)


def lag_table(length, bins, lags, factor):
    frequency = jnp.arange(1, bins + 1, dtype=jnp.int32)
    shifts = jnp.arange(lags, dtype=jnp.int32) - (lags - 1) // 2
    phase_index = jnp.mod(frequency[:, None] * shifts[None, :], length)
    angles = 2.0 * math.pi / length * phase_index.astype(jnp.float32)
    table_values = jnp.concatenate([jnp.cos(angles), -jnp.sin(angles)], axis=0) * factor
    return table_values.astype(jnp.bfloat16)


def whiten(samples, dead_flags, table_values):
    channel_count, windows, length = samples.shape
    bins = table_values.shape[1] // 2
    traces = samples.astype(jnp.float32)
    traces = traces - jnp.mean(traces, axis=-1, keepdims=True)
    tapered = (traces * taper_window(length)).astype(jnp.bfloat16)
    spectra = jnp.dot(
        tapered.reshape(channel_count * windows, length),
        table_values,
        preferred_element_type=jnp.float32,
    )
    real_part = spectra[:, :bins]
    imag_part = spectra[:, bins:]
    energy = real_part * real_part + imag_part * imag_part
    mean_energy = jnp.mean(energy, axis=-1, keepdims=True)
    inverse_scale = lax.rsqrt(energy + 0.25 * mean_energy + 1e-06)
    alive_rows = jnp.repeat((1 - dead_flags).astype(jnp.float32), windows)[:, None]
    whitened = (
        jnp.concatenate([real_part * inverse_scale, imag_part * inverse_scale], axis=1) * alive_rows
    )
    return whitened.astype(jnp.bfloat16).reshape(channel_count, windows, 2 * bins)


def correlate(receivers, sources, lag_weights):
    bins = receivers.shape[-1] // 2
    rec_values = receivers.astype(jnp.float32)
    src_values = sources.astype(jnp.float32)
    rec_re = rec_values[:, None, :, :bins]
    rec_im = rec_values[:, None, :, bins:]
    src_re = src_values[None, :, :, :bins]
    src_im = src_values[None, :, :, bins:]
    cross_re = rec_re * src_re + rec_im * src_im
    cross_im = rec_im * src_re - rec_re * src_im
    cross = jnp.concatenate([cross_re, cross_im], axis=-1).astype(jnp.bfloat16)
    result = jnp.einsum("rgwk,kl->wrgl", cross, lag_weights, preferred_element_type=jnp.float32)
    return result.astype(jnp.bfloat16)


def pick_group(source_count, rows_each):
    chosen = 1
    for candidate in range(1, source_count + 1):
        if source_count % candidate == 0 and candidate * rows_each <= 1024:
            chosen = candidate
    return chosen


def per_device(samples, dead_flags, pair_mask):
    block_size, local_windows, length = samples.shape
    table_values = forward_table(length, F)
    whitened = whiten(samples, dead_flags, table_values)
    subwin = local_windows * lax.axis_size("tm")
    lag_weights = lag_table(length, F, LAGS, 1.0 / math.sqrt(subwin * F))
    incoming = lax.all_gather(whitened, "chan", axis=0, tiled=True)
    source_count = incoming.shape[0]
    group_size = pick_group(source_count, block_size * local_windows)
    grouped = incoming.reshape(source_count // group_size, group_size, local_windows, 2 * F)

    def one_group(group_sources):
        return correlate(whitened, group_sources, lag_weights)[0]

    results = lax.map(one_group, grouped)
    placed = jnp.transpose(results, (1, 0, 2, 3)).reshape(block_size, source_count, LAGS)
    shares = lax.psum_scatter(
        placed.astype(jnp.float32).astype(jnp.bfloat16), "tm", scatter_dimension=1, tiled=True
    ).astype(jnp.float32)
    return shares * pair_mask.astype(jnp.float32)[..., None]


RADIX = 16
LANES = 128
ROWS = 8
MESH = pl.DeviceIdType.MESH


def frequency_groups(bins):
    half = RADIX // 2
    groups = []
    for residue in range(half):
        first, second = (0, half) if residue == 0 else (residue, RADIX - residue)
        all_bins = np.arange(1, bins + 1)
        groups.append((first, second, all_bins[all_bins % RADIX == first], all_bins[all_bins % RADIX == second]))
    return groups


def split_tables(length, bins):
    depth = length // RADIX
    offsets = np.arange(depth)
    columns_re, columns_im, owner, order = [], [], [], []
    for index, (first, second, bins_a, bins_b) in enumerate(frequency_groups(bins)):
        for which, chosen in ((0, bins_a), (1, bins_b)):
            for k in chosen:
                angle = 2.0 * np.pi / length * ((offsets * k) % length)
                cos, sin, zero = np.cos(angle), np.sin(angle), np.zeros(depth)
                if index == 0:
                    re = [cos, zero] if which == 0 else [zero, cos]
                    im = [-sin, zero] if which == 0 else [zero, -sin]
                elif which == 0:
                    re, im = [cos, sin], [-sin, cos]
                else:
                    re, im = [cos, -sin], [-sin, -cos]
                columns_re.append(np.concatenate(re))
                columns_im.append(np.concatenate(im))
                owner.append(index)
                order.append(k)
    tiles = bins // LANES
    table = np.zeros((tiles, 4 * depth, 2 * LANES), np.float32)
    reads = []
    for tile in range(tiles):
        owners = sorted(set(owner[tile * LANES : (tile + 1) * LANES]))
        assert len(owners) <= 2
        reads.append(tuple(owners))
        for lane in range(LANES):
            at = tile * LANES + lane
            base = owners.index(owner[at]) * 2 * depth
            table[tile, base : base + 2 * depth, lane] = columns_re[at]
            table[tile, base : base + 2 * depth, LANES + lane] = columns_im[at]
    return table, reads, np.array(order)


def ordered_lag_table(length, order, lags, factor):
    shifts = np.arange(lags) - (lags - 1) // 2
    angles = 2.0 * np.pi / length * np.mod(order[:, None] * shifts[None, :], length)
    values = np.concatenate([np.cos(angles), -np.sin(angles)], axis=0) * factor
    padded = -(-lags // LANES) * LANES
    return np.pad(values, ((0, 0), (0, padded - lags))).astype(np.float32)


def packing(block, length):
    width = block * length // ROWS
    tail = length - width
    return width, tail, width // tail if tail > 0 else 0


def packs(block, length):
    width, tail, chunks = packing(block, length)
    full = block < ROWS and block * length % (ROWS * LANES) == 0
    return full and tail % LANES == 0 and width % tail == 0 and (ROWS - block) * chunks == block


def stage_one(pieces):
    half = RADIX // 2
    sums = [pieces[a] + pieces[RADIX - a] for a in range(1, half)]
    diffs = [pieces[a] - pieces[RADIX - a] for a in range(1, half)]
    even = pieces[0] + pieces[half]
    odd = pieces[0] - pieces[half]

    def real(k):
        total = even if k % 2 == 0 else odd
        for a in range(1, half):
            total = total + sums[a - 1] * float(np.cos(2 * np.pi * a * k / RADIX))
        return total

    def imag(k):
        total = diffs[0] * float(-np.sin(2 * np.pi * k / RADIX))
        for a in range(2, half):
            total = total + diffs[a - 1] * float(-np.sin(2 * np.pi * a * k / RADIX))
        return total

    groups = [jnp.concatenate([real(0), real(half)], axis=1)]
    for k in range(1, half):
        groups.append(jnp.concatenate([real(k), imag(k)], axis=1))
    return [g.astype(jnp.bfloat16) for g in groups]


def fused_kernel(
    sizes, reads, samples_hbm, dead_hbm, mask_hbm, taper_hbm, table_ref, lag_ref, out_ref, keep_ref,
    samples_ref, dead_ref, maskv, taper_ref, packed, own, src, rec, recf, srcf, cross, table, lagv,
    table_sem, send_sem, pair_sem, fwd_sem, src_sem, rec_sem,
):
    chans, tms, block, group, bins = sizes
    me_c, me_t = lax.axis_index("chan"), lax.axis_index("tm")
    core = me_c % 2
    columns = chans // 2
    barrier = pltpu.get_barrier_semaphore()
    sibling = me_c + 1 - 2 * core
    half = group // 2
    for i in range(half):
        for w in range(tms):
            from_c = me_t * group + core * half + i

            @pl.when(jnp.logical_not(jnp.logical_and(from_c == me_c, w == me_t)))
            def _():
                pl.semaphore_signal(barrier, inc=1, device_id=(from_c, w), device_id_type=MESH)

    for step in range(1, tms):
        pl.semaphore_signal(
            barrier, inc=1, device_id=(me_c, (me_t + step) % tms), device_id_type=MESH
        )
    pl.semaphore_signal(barrier, inc=1, device_id=(sibling, me_t), device_id_type=MESH)

    load_samples = pltpu.make_async_copy(samples_hbm, samples_ref, table_sem.at[2])
    load_samples.start()
    load_dead = pltpu.make_async_copy(dead_hbm, dead_ref, table_sem.at[4])
    load_dead.start()
    load_mask = pltpu.make_async_copy(mask_hbm, maskv, table_sem.at[5])
    load_mask.start()
    load_taper = pltpu.make_async_copy(taper_hbm, taper_ref, table_sem.at[3])
    load_taper.start()
    load_table = pltpu.make_async_copy(table_ref, table, table_sem.at[0])
    load_table.start()
    load_lag = pltpu.make_async_copy(lag_ref, lagv, table_sem.at[1])
    load_lag.start()

    length = samples_ref.shape[-1]
    depth = length // RADIX
    load_samples.wait()
    load_taper.wait()
    traces = samples_ref[...].astype(jnp.float32)
    traces = traces - jnp.mean(traces, axis=-1, keepdims=True)
    tapered = (traces * taper_ref[...]).astype(jnp.bfloat16).astype(jnp.float32)
    groups = stage_one([tapered[:, a * depth : (a + 1) * depth] for a in range(RADIX)])
    load_dead.wait()
    row = lax.broadcasted_iota(jnp.int32, (block, 1), 0)
    alive = jnp.zeros((block, 1), jnp.float32)
    for r in range(block):
        alive = jnp.where(row == r, (1 - dead_ref[r]).astype(jnp.float32), alive)
    load_table.wait()
    parts = []
    energy_sum = jnp.zeros((block, LANES), jnp.float32)
    for tile, owners in enumerate(reads):
        lhs = jnp.concatenate([groups[g] for g in owners], axis=1)
        spec = jnp.dot(lhs, table[tile, : lhs.shape[1], :], preferred_element_type=jnp.float32)
        re, im = spec[:, :LANES], spec[:, LANES:]
        energy = re * re + im * im
        energy_sum = energy_sum + energy
        parts.append((re, im, energy))
    width, tail, chunks = packing(block, 2 * bins)

    def pack(start, piece):
        if start < width:
            packed[:block, start : start + LANES] = piece
            return
        for r in range(block):
            first = (r % chunks) * tail + start - width
            packed[block + r // chunks : block + r // chunks + 1, first : first + LANES] = piece[r : r + 1]

    def unpack(values, store):
        store(slice(0, block), slice(0, width), values[:block])
        for r in range(block):
            first = (r % chunks) * tail
            store(
                slice(r, r + 1), slice(width, width + tail),
                values[block + r // chunks : block + r // chunks + 1, first : first + tail],
            )

    mean_energy = jnp.sum(energy_sum, axis=-1, keepdims=True) / bins
    for tile, (re, im, energy) in enumerate(parts):
        scale = lax.rsqrt(energy + 0.25 * mean_energy + 1e-06)
        pack(tile * LANES, re * scale * alive)
        pack(bins + tile * LANES, im * scale * alive)
    own[...] = packed[...].astype(jnp.bfloat16)

    to_t = me_c // group
    slot = me_c % group
    to_half, at = slot // half, slot % half
    keeps = jnp.logical_and(to_t == me_t, to_half == core)
    pl.semaphore_wait(barrier, columns + tms - keeps.astype(jnp.int32))

    def column_at(i):
        return (me_c // 2 + columns // 2 + i) % columns

    def stays(i):
        return jnp.logical_and(keeps, column_at(i) == me_c // 2)

    def push(i):
        return pltpu.make_async_remote_copy(
            src_ref=own, dst_ref=src.at[to_half, at, me_t],
            send_sem=send_sem.at[i], recv_sem=src_sem.at[to_half, at, me_t],
            device_id=(2 * column_at(i) + to_half, to_t), device_id_type=MESH,
        )

    for i in range(columns):

        @pl.when(jnp.logical_not(stays(i)))
        def _():
            push(i).start()

        @pl.when(stays(i))
        def _():
            pltpu.make_async_copy(own, src.at[to_half, at, me_t], src_sem.at[to_half, at, me_t]).start()

    def pair_copy(step):
        return pltpu.make_async_remote_copy(
            src_ref=own, dst_ref=rec.at[me_t],
            send_sem=pair_sem.at[step], recv_sem=rec_sem.at[me_t],
            device_id=(me_c, (me_t + step) % tms), device_id_type=MESH,
        )

    for step in range(1, tms):
        pair_copy(step).start()
    own_rec = pltpu.make_async_copy(own, rec.at[me_t], pair_sem.at[0])
    own_rec.start()

    def arrival(h, i, w):
        return pltpu.make_async_copy(own, src.at[h, i, w], src_sem.at[h, i, w])

    def forward(i, w):
        return pltpu.make_async_remote_copy(
            src_ref=src.at[core, i, w], dst_ref=src.at[core, i, w],
            send_sem=fwd_sem.at[i, w], recv_sem=src_sem.at[core, i, w],
            device_id=(sibling, me_t), device_id_type=MESH,
        )

    sources = half * block
    lags = out_ref.shape[-1]

    def correlate_half(h):
        for i in range(half):
            for w in range(tms):

                def store(rows, lanes, piece):
                    srcf[w, i * block + rows.start : i * block + rows.stop, lanes] = piece

                unpack(src[h, i, w].astype(jnp.float32), store)
        for tile in range(bins // LANES):
            lanes = slice(tile * LANES, (tile + 1) * LANES)
            lanes_im = slice(bins + tile * LANES, bins + (tile + 1) * LANES)
            rec_re = [recf[w, :, lanes] for w in range(tms)]
            rec_im = [recf[w, :, lanes_im] for w in range(tms)]
            src_re = [srcf[w, :, lanes] for w in range(tms)]
            src_im = [srcf[w, :, lanes_im] for w in range(tms)]
            for r in range(block):
                total_re = total_im = None
                for w in range(tms):
                    a, c = rec_re[w][r : r + 1, :], rec_im[w][r : r + 1, :]
                    now_re = a * src_re[w] + c * src_im[w]
                    now_im = c * src_re[w] - a * src_im[w]
                    total_re = now_re if total_re is None else total_re + now_re
                    total_im = now_im if total_im is None else total_im + now_im
                cross[r * sources : (r + 1) * sources, lanes] = total_re.astype(jnp.bfloat16)
                cross[r * sources : (r + 1) * sources, lanes_im] = total_im.astype(jnp.bfloat16)
        result = jnp.dot(cross[...], lagv[...], preferred_element_type=jnp.float32)
        for r in range(block):
            out_ref[r, pl.ds(pl.multiple_of(h * sources, sources), sources), :] = result[
                r * sources : (r + 1) * sources, :lags
            ]

    for i in range(half):
        for w in range(tms):
            arrival(core, i, w).wait()
            forward(i, w).start()
    load_mask.wait()
    keep_ref[...] = maskv[...].astype(jnp.float32)
    load_lag.wait()
    own_rec.wait()
    for step in range(1, tms):
        from_t = (me_t + step) % tms
        pltpu.make_async_copy(own, rec.at[from_t], rec_sem.at[from_t]).wait()

    for w in range(tms):

        def store_rec(rows, lanes, piece):
            recf[w, rows, lanes] = piece

        unpack(rec[w].astype(jnp.float32), store_rec)

    @pl.loop(0, 2)
    def _(turn):
        @pl.when(turn == 1)
        def _():
            for i in range(half):
                for w in range(tms):
                    arrival(1 - core, i, w).wait()

        correlate_half((core + turn) % 2)

    for i in range(columns):

        @pl.when(jnp.logical_not(stays(i)))
        def _():
            push(i).wait_send()

    for step in range(1, tms):
        pair_copy(step).wait_send()
    for i in range(half):
        for w in range(tms):
            forward(i, w).wait_send()


def fused_device(chans, tms, samples, dead_flags, pair_mask):
    block, _, length = samples.shape
    sources = pair_mask.shape[1]
    group = sources // block
    table, reads, order = split_tables(length, F)
    lag_weights = ordered_lag_table(length, order, LAGS, 1.0 / math.sqrt(tms * F))
    at = np.arange(length)
    taper = (0.5 - 0.5 * np.cos(2.0 * np.pi * (at + 0.5) / length))[None, :].astype(np.float32)
    vmem, hbm = pl.BlockSpec(memory_space=pltpu.VMEM), pl.BlockSpec(memory_space=pltpu.HBM)
    sem = pltpu.SemaphoreType.DMA
    half = group // 2
    width = packing(block, 2 * F)[0]
    result, keep = pl.pallas_call(
        functools.partial(fused_kernel, (chans, tms, block, group, F), reads),
        out_shape=[
            pltpu.VMEM((block, sources, LAGS), jnp.float32),
            pltpu.VMEM((block, sources), jnp.float32),
        ],
        in_specs=[hbm] * 6,
        out_specs=[vmem] * 2,
        scratch_shapes=[
            pltpu.VMEM((block, length), jnp.bfloat16),
            pltpu.SMEM((block,), jnp.int32),
            pltpu.VMEM((block, sources), jnp.int32),
            pltpu.VMEM((1, length), jnp.float32),
            pltpu.VMEM((ROWS, width), jnp.float32),
            pltpu.VMEM((ROWS, width), jnp.bfloat16),
            pltpu.VMEM((2, half, tms, ROWS, width), jnp.bfloat16),
            pltpu.VMEM((tms, ROWS, width), jnp.bfloat16),
            pltpu.VMEM((tms, block, 2 * F), jnp.float32),
            pltpu.VMEM((tms, half * block, 2 * F), jnp.float32),
            pltpu.VMEM((block * half * block, 2 * F), jnp.bfloat16),
            pltpu.VMEM(table.shape, jnp.bfloat16),
            pltpu.VMEM(lag_weights.shape, jnp.bfloat16),
            sem((6,)), sem((chans // 2,)), sem((tms,)), sem((half, tms)), sem((2, half, tms)), sem((tms,)),
        ],
        compiler_params=pltpu.CompilerParams(
            collective_id=0, has_side_effects=True, vmem_limit_bytes=24 * 1024 * 1024
        ),
    )(
        *(
            pltpu.with_memory_space_constraint(operand, pltpu.HBM)
            for operand in (
                samples.reshape(block, length), dead_flags, pair_mask, jnp.asarray(taper),
                jnp.asarray(table, jnp.bfloat16), jnp.asarray(lag_weights, jnp.bfloat16),
            )
        )
    )
    return result * keep[..., None]


def dispatch(chans, tms, samples, dead_flags, pair_mask):
    block, windows, length = samples.shape
    sources = pair_mask.shape[1]
    whole_blocks = sources % (2 * block) == 0 and chans % 2 == 0 and sources % 16 == 0 and block * chans == sources * tms
    aligned = length == RADIX * LANES and F % LANES == 0 and windows == 1
    if whole_blocks and aligned and packs(block, 2 * F):
        return fused_device(chans, tms, samples, dead_flags, pair_mask)
    return per_device(samples, dead_flags, pair_mask)


def solution(mesh):
    in_specs = (P("chan", "tm", None), P("chan"), P("chan", "tm"))
    out_specs = P("chan", "tm", None)
    chans, tms = mesh.shape["chan"], mesh.shape["tm"]
    return jax.shard_map(
        functools.partial(dispatch, chans, tms),
        mesh=mesh, in_specs=in_specs, out_specs=out_specs, check_vma=False,
    )
```

```python
import functools
import math

import jax
import jax.numpy as jnp
import numpy as np
from jax import lax
from jax.experimental import pallas as pl
from jax.experimental.pallas import tpu as pltpu
from jax.sharding import PartitionSpec as P

F = 768
LAGS = 301


def taper_window(length):
    sample_index = jnp.arange(length, dtype=jnp.float32)
    return 0.5 - 0.5 * jnp.cos(2.0 * math.pi * (sample_index + 0.5) / length)


def forward_table(length, bins):
    sample_index = jnp.arange(length, dtype=jnp.int32)
    frequency = jnp.arange(1, bins + 1, dtype=jnp.int32)
    phase_index = sample_index[:, None] * frequency[None, :] % length
    angles = 2.0 * math.pi / length * phase_index.astype(jnp.float32)
    return jnp.concatenate([jnp.cos(angles), -jnp.sin(angles)], axis=1).astype(jnp.bfloat16)


def lag_table(length, bins, lags, factor):
    frequency = jnp.arange(1, bins + 1, dtype=jnp.int32)
    shifts = jnp.arange(lags, dtype=jnp.int32) - (lags - 1) // 2
    phase_index = jnp.mod(frequency[:, None] * shifts[None, :], length)
    angles = 2.0 * math.pi / length * phase_index.astype(jnp.float32)
    table_values = jnp.concatenate([jnp.cos(angles), -jnp.sin(angles)], axis=0) * factor
    return table_values.astype(jnp.bfloat16)


def whiten(samples, dead_flags, table_values):
    channel_count, windows, length = samples.shape
    bins = table_values.shape[1] // 2
    traces = samples.astype(jnp.float32)
    traces = traces - jnp.mean(traces, axis=-1, keepdims=True)
    tapered = (traces * taper_window(length)).astype(jnp.bfloat16)
    spectra = jnp.dot(
        tapered.reshape(channel_count * windows, length),
        table_values,
        preferred_element_type=jnp.float32,
    )
    real_part = spectra[:, :bins]
    imag_part = spectra[:, bins:]
    energy = real_part * real_part + imag_part * imag_part
    mean_energy = jnp.mean(energy, axis=-1, keepdims=True)
    inverse_scale = lax.rsqrt(energy + 0.25 * mean_energy + 1e-06)
    alive_rows = jnp.repeat((1 - dead_flags).astype(jnp.float32), windows)[:, None]
    whitened = (
        jnp.concatenate([real_part * inverse_scale, imag_part * inverse_scale], axis=1) * alive_rows
    )
    return whitened.astype(jnp.bfloat16).reshape(channel_count, windows, 2 * bins)


def correlate(receivers, sources, lag_weights):
    bins = receivers.shape[-1] // 2
    rec_values = receivers.astype(jnp.float32)
    src_values = sources.astype(jnp.float32)
    rec_re = rec_values[:, None, :, :bins]
    rec_im = rec_values[:, None, :, bins:]
    src_re = src_values[None, :, :, :bins]
    src_im = src_values[None, :, :, bins:]
    cross_re = rec_re * src_re + rec_im * src_im
    cross_im = rec_im * src_re - rec_re * src_im
    cross = jnp.concatenate([cross_re, cross_im], axis=-1).astype(jnp.bfloat16)
    result = jnp.einsum("rgwk,kl->wrgl", cross, lag_weights, preferred_element_type=jnp.float32)
    return result.astype(jnp.bfloat16)


def pick_group(source_count, rows_each):
    chosen = 1
    for candidate in range(1, source_count + 1):
        if source_count % candidate == 0 and candidate * rows_each <= 1024:
            chosen = candidate
    return chosen


def per_device(samples, dead_flags, pair_mask):
    block_size, local_windows, length = samples.shape
    table_values = forward_table(length, F)
    whitened = whiten(samples, dead_flags, table_values)
    subwin = local_windows * lax.axis_size("tm")
    lag_weights = lag_table(length, F, LAGS, 1.0 / math.sqrt(subwin * F))
    incoming = lax.all_gather(whitened, "chan", axis=0, tiled=True)
    source_count = incoming.shape[0]
    group_size = pick_group(source_count, block_size * local_windows)
    grouped = incoming.reshape(source_count // group_size, group_size, local_windows, 2 * F)

    def one_group(group_sources):
        return correlate(whitened, group_sources, lag_weights)[0]

    results = lax.map(one_group, grouped)
    placed = jnp.transpose(results, (1, 0, 2, 3)).reshape(block_size, source_count, LAGS)
    shares = lax.psum_scatter(
        placed.astype(jnp.float32).astype(jnp.bfloat16), "tm", scatter_dimension=1, tiled=True
    ).astype(jnp.float32)
    return shares * pair_mask.astype(jnp.float32)[..., None]


RADIX = 16
LANES = 128
ROWS = 8
MESH = pl.DeviceIdType.MESH


def frequency_groups(bins):
    half = RADIX // 2
    groups = []
    for residue in range(half):
        first, second = (0, half) if residue == 0 else (residue, RADIX - residue)
        all_bins = np.arange(1, bins + 1)
        groups.append((first, second, all_bins[all_bins % RADIX == first], all_bins[all_bins % RADIX == second]))
    return groups


def split_tables(length, bins):
    depth = length // RADIX
    offsets = np.arange(depth)
    columns_re, columns_im, owner, order = [], [], [], []
    for index, (first, second, bins_a, bins_b) in enumerate(frequency_groups(bins)):
        for which, chosen in ((0, bins_a), (1, bins_b)):
            for k in chosen:
                angle = 2.0 * np.pi / length * ((offsets * k) % length)
                cos, sin, zero = np.cos(angle), np.sin(angle), np.zeros(depth)
                if index == 0:
                    re = [cos, zero] if which == 0 else [zero, cos]
                    im = [-sin, zero] if which == 0 else [zero, -sin]
                elif which == 0:
                    re, im = [cos, sin], [-sin, cos]
                else:
                    re, im = [cos, -sin], [-sin, -cos]
                columns_re.append(np.concatenate(re))
                columns_im.append(np.concatenate(im))
                owner.append(index)
                order.append(k)
    tiles = bins // LANES
    table = np.zeros((tiles, 4 * depth, 2 * LANES), np.float32)
    reads = []
    for tile in range(tiles):
        owners = sorted(set(owner[tile * LANES : (tile + 1) * LANES]))
        assert len(owners) <= 2
        reads.append(tuple(owners))
        for lane in range(LANES):
            at = tile * LANES + lane
            base = owners.index(owner[at]) * 2 * depth
            table[tile, base : base + 2 * depth, lane] = columns_re[at]
            table[tile, base : base + 2 * depth, LANES + lane] = columns_im[at]
    return table, reads, np.array(order)


def ordered_lag_table(length, order, lags, factor):
    shifts = np.arange(lags) - (lags - 1) // 2
    angles = 2.0 * np.pi / length * np.mod(order[:, None] * shifts[None, :], length)
    values = np.concatenate([np.cos(angles), -np.sin(angles)], axis=0) * factor
    padded = -(-lags // LANES) * LANES
    return np.pad(values, ((0, 0), (0, padded - lags))).astype(np.float32)


def packing(block, length):
    width = block * length // ROWS
    tail = length - width
    return width, tail, width // tail if tail > 0 else 0


def packs(block, length):
    width, tail, chunks = packing(block, length)
    full = block < ROWS and block * length % (ROWS * LANES) == 0
    return full and tail % LANES == 0 and width % tail == 0 and (ROWS - block) * chunks == block


def stage_one(pieces):
    half = RADIX // 2
    sums = [pieces[a] + pieces[RADIX - a] for a in range(1, half)]
    diffs = [pieces[a] - pieces[RADIX - a] for a in range(1, half)]
    even = pieces[0] + pieces[half]
    odd = pieces[0] - pieces[half]

    def real(k):
        total = even if k % 2 == 0 else odd
        for a in range(1, half):
            total = total + sums[a - 1] * float(np.cos(2 * np.pi * a * k / RADIX))
        return total

    def imag(k):
        total = diffs[0] * float(-np.sin(2 * np.pi * k / RADIX))
        for a in range(2, half):
            total = total + diffs[a - 1] * float(-np.sin(2 * np.pi * a * k / RADIX))
        return total

    groups = [jnp.concatenate([real(0), real(half)], axis=1)]
    for k in range(1, half):
        groups.append(jnp.concatenate([real(k), imag(k)], axis=1))
    return [g.astype(jnp.bfloat16) for g in groups]


def fused_kernel(
    sizes, reads, samples_hbm, dead_hbm, mask_hbm, taper_hbm, table_ref, lag_ref, out_ref, keep_ref,
    samples_ref, dead_ref, maskv, taper_ref, packed, own, src, rec, recf, srcf, cross, table, lagv,
    table_sem, send_sem, pair_sem, fwd_sem, src_sem, rec_sem,
):
    chans, tms, block, group, bins = sizes
    me_c, me_t = lax.axis_index("chan"), lax.axis_index("tm")
    core = me_c % 2
    columns = chans // 2
    barrier = pltpu.get_barrier_semaphore()
    sibling = me_c + 1 - 2 * core
    half = group // 2
    for i in range(half):
        for w in range(tms):
            from_c = me_t * group + core * half + i

            @pl.when(jnp.logical_not(jnp.logical_and(from_c == me_c, w == me_t)))
            def _():
                pl.semaphore_signal(barrier, inc=1, device_id=(from_c, w), device_id_type=MESH)

    for step in range(1, tms):
        pl.semaphore_signal(
            barrier, inc=1, device_id=(me_c, (me_t + step) % tms), device_id_type=MESH
        )
    pl.semaphore_signal(barrier, inc=1, device_id=(sibling, me_t), device_id_type=MESH)

    load_samples = pltpu.make_async_copy(samples_hbm, samples_ref, table_sem.at[2])
    load_samples.start()
    load_dead = pltpu.make_async_copy(dead_hbm, dead_ref, table_sem.at[4])
    load_dead.start()
    load_mask = pltpu.make_async_copy(mask_hbm, maskv, table_sem.at[5])
    load_mask.start()
    load_taper = pltpu.make_async_copy(taper_hbm, taper_ref, table_sem.at[3])
    load_taper.start()
    load_table = pltpu.make_async_copy(table_ref, table, table_sem.at[0])
    load_table.start()
    load_lag = pltpu.make_async_copy(lag_ref, lagv, table_sem.at[1])
    load_lag.start()

    length = samples_ref.shape[-1]
    depth = length // RADIX
    load_samples.wait()
    load_taper.wait()
    traces = samples_ref[...].astype(jnp.float32)
    traces = traces - jnp.mean(traces, axis=-1, keepdims=True)
    tapered = (traces * taper_ref[...]).astype(jnp.bfloat16).astype(jnp.float32)
    groups = stage_one([tapered[:, a * depth : (a + 1) * depth] for a in range(RADIX)])
    load_dead.wait()
    row = lax.broadcasted_iota(jnp.int32, (block, 1), 0)
    alive = jnp.zeros((block, 1), jnp.float32)
    for r in range(block):
        alive = jnp.where(row == r, (1 - dead_ref[r]).astype(jnp.float32), alive)
    load_table.wait()
    parts = []
    energy_sum = jnp.zeros((block, LANES), jnp.float32)
    for tile, owners in enumerate(reads):
        lhs = jnp.concatenate([groups[g] for g in owners], axis=1)
        spec = jnp.dot(lhs, table[tile, : lhs.shape[1], :], preferred_element_type=jnp.float32)
        re, im = spec[:, :LANES], spec[:, LANES:]
        energy = re * re + im * im
        energy_sum = energy_sum + energy
        parts.append((re, im, energy))
    width, tail, chunks = packing(block, 2 * bins)

    def pack(start, piece):
        if start < width:
            packed[:block, start : start + LANES] = piece
            return
        for r in range(block):
            first = (r % chunks) * tail + start - width
            packed[block + r // chunks : block + r // chunks + 1, first : first + LANES] = piece[r : r + 1]

    def unpack(values, store):
        store(slice(0, block), slice(0, width), values[:block])
        for r in range(block):
            first = (r % chunks) * tail
            store(
                slice(r, r + 1), slice(width, width + tail),
                values[block + r // chunks : block + r // chunks + 1, first : first + tail],
            )

    mean_energy = jnp.sum(energy_sum, axis=-1, keepdims=True) / bins
    for tile, (re, im, energy) in enumerate(parts):
        scale = lax.rsqrt(energy + 0.25 * mean_energy + 1e-06)
        pack(tile * LANES, re * scale * alive)
        pack(bins + tile * LANES, im * scale * alive)
    own[...] = packed[...].astype(jnp.bfloat16)

    to_t = me_c // group
    slot = me_c % group
    to_half, at = slot // half, slot % half
    keeps = jnp.logical_and(to_t == me_t, to_half == core)
    pl.semaphore_wait(barrier, columns + tms - keeps.astype(jnp.int32))

    def column_at(i):
        return (me_c // 2 + i) % columns

    def stays(i):
        return jnp.logical_and(keeps, column_at(i) == me_c // 2)

    def push(i):
        return pltpu.make_async_remote_copy(
            src_ref=own, dst_ref=src.at[to_half, at, me_t],
            send_sem=send_sem.at[i], recv_sem=src_sem.at[to_half, at, me_t],
            device_id=(2 * column_at(i) + to_half, to_t), device_id_type=MESH,
        )

    for i in range(columns):

        @pl.when(jnp.logical_not(stays(i)))
        def _():
            push(i).start()

        @pl.when(stays(i))
        def _():
            pltpu.make_async_copy(own, src.at[to_half, at, me_t], src_sem.at[to_half, at, me_t]).start()

    def pair_copy(step):
        return pltpu.make_async_remote_copy(
            src_ref=own, dst_ref=rec.at[me_t],
            send_sem=pair_sem.at[step], recv_sem=rec_sem.at[me_t],
            device_id=(me_c, (me_t + step) % tms), device_id_type=MESH,
        )

    for step in range(1, tms):
        pair_copy(step).start()
    own_rec = pltpu.make_async_copy(own, rec.at[me_t], pair_sem.at[0])
    own_rec.start()

    def arrival(h, i, w):
        return pltpu.make_async_copy(own, src.at[h, i, w], src_sem.at[h, i, w])

    def forward(i, w):
        return pltpu.make_async_remote_copy(
            src_ref=src.at[core, i, w], dst_ref=src.at[core, i, w],
            send_sem=fwd_sem.at[i, w], recv_sem=src_sem.at[core, i, w],
            device_id=(sibling, me_t), device_id_type=MESH,
        )

    sources = half * block
    lags = out_ref.shape[-1]

    def correlate_half(h):
        for i in range(half):
            for w in range(tms):

                def store(rows, lanes, piece):
                    srcf[w, i * block + rows.start : i * block + rows.stop, lanes] = piece

                unpack(src[h, i, w].astype(jnp.float32), store)
        for tile in range(bins // LANES):
            lanes = slice(tile * LANES, (tile + 1) * LANES)
            lanes_im = slice(bins + tile * LANES, bins + (tile + 1) * LANES)
            rec_re = [recf[w, :, lanes] for w in range(tms)]
            rec_im = [recf[w, :, lanes_im] for w in range(tms)]
            src_re = [srcf[w, :, lanes] for w in range(tms)]
            src_im = [srcf[w, :, lanes_im] for w in range(tms)]
            for r in range(block):
                total_re = total_im = None
                for w in range(tms):
                    a, c = rec_re[w][r : r + 1, :], rec_im[w][r : r + 1, :]
                    now_re = a * src_re[w] + c * src_im[w]
                    now_im = c * src_re[w] - a * src_im[w]
                    total_re = now_re if total_re is None else total_re + now_re
                    total_im = now_im if total_im is None else total_im + now_im
                cross[r * sources : (r + 1) * sources, lanes] = total_re.astype(jnp.bfloat16)
                cross[r * sources : (r + 1) * sources, lanes_im] = total_im.astype(jnp.bfloat16)
        result = jnp.dot(cross[...], lagv[...], preferred_element_type=jnp.float32)
        for r in range(block):
            out_ref[r, pl.ds(pl.multiple_of(h * sources, sources), sources), :] = result[
                r * sources : (r + 1) * sources, :lags
            ]

    for i in range(half):
        for w in range(tms):
            arrival(core, i, w).wait()
            forward(i, w).start()
    load_mask.wait()
    keep_ref[...] = maskv[...].astype(jnp.float32)
    load_lag.wait()
    own_rec.wait()
    for step in range(1, tms):
        from_t = (me_t + step) % tms
        pltpu.make_async_copy(own, rec.at[from_t], rec_sem.at[from_t]).wait()

    for w in range(tms):

        def store_rec(rows, lanes, piece):
            recf[w, rows, lanes] = piece

        unpack(rec[w].astype(jnp.float32), store_rec)

    @pl.loop(0, 2)
    def _(turn):
        @pl.when(turn == 1)
        def _():
            for i in range(half):
                for w in range(tms):
                    arrival(1 - core, i, w).wait()

        correlate_half((core + turn) % 2)

    for i in range(columns):

        @pl.when(jnp.logical_not(stays(i)))
        def _():
            push(i).wait_send()

    for step in range(1, tms):
        pair_copy(step).wait_send()
    for i in range(half):
        for w in range(tms):
            forward(i, w).wait_send()


def fused_device(chans, tms, samples, dead_flags, pair_mask):
    block, _, length = samples.shape
    sources = pair_mask.shape[1]
    group = sources // block
    table, reads, order = split_tables(length, F)
    lag_weights = ordered_lag_table(length, order, LAGS, 1.0 / math.sqrt(tms * F))
    at = np.arange(length)
    taper = (0.5 - 0.5 * np.cos(2.0 * np.pi * (at + 0.5) / length))[None, :].astype(np.float32)
    vmem, hbm = pl.BlockSpec(memory_space=pltpu.VMEM), pl.BlockSpec(memory_space=pltpu.HBM)
    sem = pltpu.SemaphoreType.DMA
    half = group // 2
    width = packing(block, 2 * F)[0]
    result, keep = pl.pallas_call(
        functools.partial(fused_kernel, (chans, tms, block, group, F), reads),
        out_shape=[
            pltpu.VMEM((block, sources, LAGS), jnp.float32),
            pltpu.VMEM((block, sources), jnp.float32),
        ],
        in_specs=[hbm] * 6,
        out_specs=[vmem] * 2,
        scratch_shapes=[
            pltpu.VMEM((block, length), jnp.bfloat16),
            pltpu.SMEM((block,), jnp.int32),
            pltpu.VMEM((block, sources), jnp.int32),
            pltpu.VMEM((1, length), jnp.float32),
            pltpu.VMEM((ROWS, width), jnp.float32),
            pltpu.VMEM((ROWS, width), jnp.bfloat16),
            pltpu.VMEM((2, half, tms, ROWS, width), jnp.bfloat16),
            pltpu.VMEM((tms, ROWS, width), jnp.bfloat16),
            pltpu.VMEM((tms, block, 2 * F), jnp.float32),
            pltpu.VMEM((tms, half * block, 2 * F), jnp.float32),
            pltpu.VMEM((block * half * block, 2 * F), jnp.bfloat16),
            pltpu.VMEM(table.shape, jnp.bfloat16),
            pltpu.VMEM(lag_weights.shape, jnp.bfloat16),
            sem((6,)), sem((chans // 2,)), sem((tms,)), sem((half, tms)), sem((2, half, tms)), sem((tms,)),
        ],
        compiler_params=pltpu.CompilerParams(
            collective_id=0, has_side_effects=True, vmem_limit_bytes=24 * 1024 * 1024
        ),
    )(
        *(
            pltpu.with_memory_space_constraint(operand, pltpu.HBM)
            for operand in (
                samples.reshape(block, length), dead_flags, pair_mask, jnp.asarray(taper),
                jnp.asarray(table, jnp.bfloat16), jnp.asarray(lag_weights, jnp.bfloat16),
            )
        )
    )
    return result * keep[..., None]


def dispatch(chans, tms, samples, dead_flags, pair_mask):
    block, windows, length = samples.shape
    sources = pair_mask.shape[1]
    whole_blocks = sources % (2 * block) == 0 and chans % 2 == 0 and sources % 16 == 0 and block * chans == sources * tms
    aligned = length == RADIX * LANES and F % LANES == 0 and windows == 1
    if whole_blocks and aligned and packs(block, 2 * F):
        return fused_device(chans, tms, samples, dead_flags, pair_mask)
    return per_device(samples, dead_flags, pair_mask)


def solution(mesh):
    in_specs = (P("chan", "tm", None), P("chan"), P("chan", "tm"))
    out_specs = P("chan", "tm", None)
    chans, tms = mesh.shape["chan"], mesh.shape["tm"]
    return jax.shard_map(
        functools.partial(dispatch, chans, tms),
        mesh=mesh, in_specs=in_specs, out_specs=out_specs, check_vma=False,
    )
```
